128 devices in a mesh: tm: 8 (over x, core), member: 16 (over z, y).
Axes of the slice: x: 4, y: 4, z: 4, core: 2. Of those that a mesh axis runs over, the one named last changes fastest.
Arguments:
- sensors: bfloat16 [16, 2048, 256], P('member', 'tm'), may hold values from -6 to 6
- kernel: bfloat16 [256, 256, 512], P('member'), may hold values from -0.0234375 to 0.0234375
- target: bfloat16 [16, 2048, 512], P('member', 'tm'), may hold values from -15 to 15
Outputs:
- errors: bfloat16 [16, 2048, 512], P('member', 'tm')
- whiteness: float32 [64, 512], replicated
The draws below stay inside these ranges and needn't reach their ends.
All inputs are finite; a program needn't handle non-finite values.
Results may differ from the reference program's by a relative error of at most 0.0018.
Values may be sent and summed in bfloat16 or wider, within the bound.
No kernel may reach another device: no remote copies, remote signals or barrier semaphores. Data moves between devices by JAX's collectives and lax.ppermute only.
A program may use at most 64 MiB of HBM per device.

```python
import math
import jax
import jax.numpy as jnp
from jax import lax

C = 256
M = 512
L = 256
LAGS = 64
TIME = 2048
MEMBERS = 16


def draw_target(key, part):
    base_key = jax.random.fold_in(jax.random.fold_in(key, 11), 1)
    times = jnp.arange(TIME, dtype=jnp.float32) / float(TIME)
    base = jnp.clip(jax.random.normal(base_key, (MEMBERS, TIME, M), jnp.float32), -5.0, 5.0)
    values = base * (1.0 + 2.0 * times)[None, :, None]
    return values.astype(jnp.bfloat16)


def level_of(stream_key, extent, cuts, least, high):
    level = 1.0
    for dim, shards_of in cuts:
        heights = jax.random.uniform(jax.random.fold_in(jax.random.fold_in(stream_key, 6), dim), (shards_of,), jnp.float32, least / len(cuts), high / len(cuts))
        level = level * jnp.repeat(jnp.exp(heights), extent[dim] // shards_of).reshape((-1,) + (1,) * (len(extent) - 1 - dim))
    return level


def gaussian(stream_key, shape, scale, most, cuts=(), held_as=jnp.bfloat16):
    result = scale * jax.random.normal(stream_key, shape, jnp.float32)
    if cuts:
        result = result * level_of(stream_key, shape, cuts, -0.22, 0.18)
    return jnp.clip(result, -most, most).astype(held_as)


def setup_inputs(seed: int = 0) -> dict:
    arg_keys = jax.random.split(jax.random.key(seed), 4)
    sensors = gaussian(arg_keys[0], (MEMBERS, TIME, C), 1.0, 6.0, ((0, 16), (1, 8)))
    kernel = gaussian(arg_keys[1], (L, C, M), (L * C) ** -0.5, 0.0234375, ((0, 16),))
    target = draw_target(jax.random.fold_in(arg_keys[3], 71), 0)
    return dict(sensors=sensors, kernel=kernel, target=target)


EPS = 1e-06

def member_estimate(member_signal, kernel):
    padded = jnp.concatenate([jnp.zeros((L, C), member_signal.dtype), member_signal], axis=0)

    def add_block(running, block_index):
        base = (L - block_index * 16 - 15).astype(jnp.int32)
        block = lax.dynamic_slice_in_dim(padded, base, TIME + 15, 0)
        kernel_block = lax.dynamic_slice_in_dim(kernel, (block_index * 16).astype(jnp.int32), 16, 0)
        for inner in range(16):
            window = block[15 - inner:15 - inner + TIME]
            running = running + jnp.dot(window, kernel_block[inner], preferred_element_type=jnp.float32)
        return (running, None)
    start = jnp.zeros((TIME, M), jnp.float32)
    running, _ = lax.scan(add_block, start, jnp.arange(L // 16, dtype=jnp.int32))
    return running

def reference(sensors, kernel, target):
    estimate = lax.map(lambda member_signal: member_estimate(member_signal, kernel), sensors)
    error_field = target.astype(jnp.float32) - estimate
    errors = error_field.astype(jnp.bfloat16)
    padded = jnp.concatenate([jnp.zeros((MEMBERS, LAGS, M), jnp.float32), error_field], axis=1)

    def lag_sum(lag_index):
        window = lax.dynamic_slice_in_dim(padded, (LAGS - lag_index).astype(jnp.int32), TIME, 1)
        return lax.optimization_barrier(jnp.sum(error_field * window, axis=(0, 1)))
    lag_partial = lax.map(lag_sum, jnp.arange(LAGS + 1, dtype=jnp.int32))
    sample_count = float(MEMBERS * TIME)
    whiteness = math.sqrt(sample_count) * (lag_partial[1:] / sample_count) / (lag_partial[0] / sample_count + EPS)
    return (errors, whiteness)
```

```python
import functools
import math

import jax
import jax.numpy as jnp
from jax import lax
from jax.experimental import pallas as pl
from jax.experimental.pallas import tpu as pltpu
from jax.sharding import Mesh
from jax.sharding import PartitionSpec as P

LAGS = 64
EPS = 1e-06

NX, NC, NZ, NY = 4, 2, 4, 4
R = 8
J = 32
RJ = R * J
CH = 128
TB = 256
TAU = TB // R
SLOTS = 16
KL = 256
ND = KL // R + 1
PADL = 128
KW = PADL + ND * RJ
PX = R * CH


F32 = jnp.float32
BF16 = jnp.bfloat16
VMEM = pltpu.VMEM
ANY = pl.ANY


def smem_spec():
    return pl.BlockSpec(memory_space=pltpu.SMEM)


def vmem_spec():
    return pl.BlockSpec(memory_space=pltpu.VMEM)


def prep_sensors_kernel(idx, s_ref, own_ref, oth_ref, f_ref):
    c = idx[1]
    f_ref[0] = s_ref[0, :, :CH].astype(F32)
    f_ref[1] = s_ref[0, :, CH:].astype(F32)
    for p in range(R):
        lo = f_ref[0, pl.ds(p, TAU, stride=R), :]
        hi = f_ref[1, pl.ds(p, TAU, stride=R), :]
        first = c == 0
        own_ref[:, p * CH : (p + 1) * CH] = jnp.where(first, lo, hi).astype(BF16)
        oth_ref[:, p * CH : (p + 1) * CH] = jnp.where(first, hi, lo).astype(BF16)


def prep_sensors(idx, s):
    return pl.pallas_call(
        prep_sensors_kernel,
        out_shape=(jax.ShapeDtypeStruct((TAU, PX), BF16),) * 2,
        in_specs=[smem_spec(), vmem_spec()],
        out_specs=(vmem_spec(), vmem_spec()),
        scratch_shapes=[VMEM((2, TB, CH), F32)],
        name="prep_sensors",
    )(idx, s)


def prep_kernel_kernel(idx, k_ref, o_ref):
    x = idx[0]
    row = lax.broadcasted_iota(jnp.int32, (128, 128), 0)
    col = lax.broadcasted_iota(jnp.int32, (128, 128), 1)
    pick = [
        jnp.where((row - x * J == col - i * J) & (col >= i * J) & (col < (i + 1) * J), 1.0, 0.0).astype(BF16)
        for i in range(4)
    ]
    for y in range(NY):
        out = jnp.zeros((CH, 128), F32)
        for i in range(4):
            out = out + jnp.dot(
                k_ref[i, :, y * 128 : (y + 1) * 128], pick[i], preferred_element_type=F32
            )
        o_ref[y] = out.astype(BF16)


def prep_kernel(idx, k):
    return pl.pallas_call(
        prep_kernel_kernel,
        out_shape=jax.ShapeDtypeStruct((NY, CH, 16 * J), BF16),
        grid_spec=pltpu.PrefetchScalarGridSpec(
            num_scalar_prefetch=1,
            grid=(4,),
            in_specs=[pl.BlockSpec((4, CH, 512), lambda q, idx: (q, idx[1], 0))],
            out_specs=pl.BlockSpec((NY, CH, 128), lambda q, idx: (0, 0, q)),
        ),
        name="prep_kernel",
    )(idx, k)


def lane_groups(shape):
    return lax.broadcasted_iota(jnp.int32, shape, len(shape) - 1) // J


def regroup(blocks, group):
    out = []
    for a in range(4):
        acc = None
        for g in range(4):
            shift = (g - a) * J % 128
            v = blocks[g] if shift == 0 else pltpu.roll(blocks[g], shift, 1)
            acc = v if acc is None else jnp.where(group == g, v, acc)
        out.append(acc)
    return out


def prep_target_kernel(t_ref, o_ref, f_ref):
    for y in range(NY):
        f_ref[...] = t_ref[0, :, y * 128 : (y + 1) * 128].astype(F32)
        group = lane_groups((TAU, 128))
        for q in range(2):
            rows = [f_ref[pl.ds(4 * q + i, TAU, stride=R), :] for i in range(4)]
            for x, v in enumerate(regroup(rows, group)):
                o_ref[y * NX + x, :, q * 128 : (q + 1) * 128] = v.astype(BF16)


def prep_target(t):
    return pl.pallas_call(
        prep_target_kernel,
        out_shape=jax.ShapeDtypeStruct((SLOTS, TAU, RJ), BF16),
        in_specs=[vmem_spec()],
        out_specs=vmem_spec(),
        scratch_shapes=[VMEM((TB, 128), F32)],
        name="prep_target",
    )(t)


def main_kernel(idx, *refs):
    x_refs = refs[0:4]
    k_refs = refs[4:8]
    keep_ref, send_ref = refs[8:10]
    a_ref, f_ref, xr_ref, kr_ref, kk_ref, sem_x, sem_k = refs[10:]
    x, c, z, y = idx[0], idx[1], idx[2], idx[3]

    copies_k = []
    for d in range(NZ):
        zs = lax.rem(z + NZ - d, NZ)
        for yy in range(NY):
            at = pl.multiple_of(256 + (zs * NY + yy) * 512, 128)
            cp = pltpu.make_async_copy(
                k_refs[d].at[yy], kr_ref.at[:, pl.ds(at, 512)], sem_k.at[d, yy]
            )
            cp.start()
            copies_k.append(cp)
    copies_x = []
    for d in range(NY):
        ys = lax.rem(y + NY - d, NY)
        for e in range(NX):
            xs = lax.rem(x + NX - e, NX)
            cp = pltpu.make_async_copy(x_refs[d].at[e], a_ref.at[ys * NX + xs], sem_x.at[d, e])
            cp.start()
            copies_x.append(cp)

    kr_ref[:, 0:256] = jnp.zeros((CH, 256), BF16)
    kr_ref[:, 256 + KL * J :] = jnp.zeros((CH, 384), BF16)
    row = lax.broadcasted_iota(jnp.int32, (256, 384), 0)
    col = lax.broadcasted_iota(jnp.int32, (256, 384), 1)
    s = col // 128 + 1
    shifter = jnp.where(row == 128 + col % 128 - J * s, 1.0, 0.0).astype(BF16)
    for cp in copies_k:
        cp.wait()

    def shift_block(q, _):
        at = pl.multiple_of(q * 128, 128)
        two = kr_ref[:, pl.ds(at, 256)]
        moved = jnp.dot(two, shifter, preferred_element_type=F32).astype(BF16)
        kk_ref[0:CH, pl.ds(at, 128)] = two[:, 128:]
        for s in range(3):
            kk_ref[(s + 1) * CH : (s + 2) * CH, pl.ds(at, 128)] = moved[:, s * 128 : (s + 1) * 128]
        return 0

    lax.fori_loop(0, KW // 128, shift_block, 0)

    for cp in copies_x:
        cp.wait()
    half = TAU * SLOTS
    first = lax.broadcasted_iota(jnp.int32, (half, 128), 0) % NX == 0
    for b in range(PX // 128):
        lanes = slice(b * 128, (b + 1) * 128)
        for i in range(SLOTS):
            f_ref[b, pl.ds(i, 2 * TAU, stride=SLOTS), :] = a_ref[i, :, lanes].astype(F32)
        xr_ref[half:, lanes] = f_ref[b].astype(BF16)
        prior = f_ref[b, half - 1 : 2 * half - 1, :]
        xr_ref[0:half, lanes] = jnp.where(first, 0.0, prior).astype(BF16)

    for out_ref, cc in ((send_ref, 1 - c), (keep_ref, c)):
        out_ref[...] = jnp.zeros((half, RJ), F32)

        def step(d, _, out_ref=out_ref, cc=cc):
            r0 = pl.multiple_of((TAU + cc * TAU - d) * SLOTS, SLOTS)
            at = pl.multiple_of(d * RJ, 128)
            out_ref[...] += jnp.dot(
                xr_ref[pl.ds(r0, half), : PX // 2],
                kk_ref[:, pl.ds(at + PADL, RJ)],
                preferred_element_type=F32,
            ) + jnp.dot(
                xr_ref[pl.ds(r0, half), PX // 2 :],
                kk_ref[:, pl.ds(at, RJ)],
                preferred_element_type=F32,
            )
            return 0

        lax.fori_loop(0, ND, step, 0)


def main(idx, xs, ks):
    half = TAU * SLOTS
    return pl.pallas_call(
        main_kernel,
        out_shape=(jax.ShapeDtypeStruct((half, RJ), F32),) * 2,
        in_specs=[smem_spec()] + [pl.BlockSpec(memory_space=ANY)] * 8,
        out_specs=(vmem_spec(), vmem_spec()),
        scratch_shapes=[
            VMEM((SLOTS, 2 * TAU, PX), BF16),
            VMEM((PX // 128, 2 * half, 128), F32),
            VMEM((3 * half, PX), BF16),
            VMEM((CH, KW + 256 - 128 + 128), BF16),
            VMEM((4 * CH, KW), BF16),
            pltpu.SemaphoreType.DMA((4, 4)),
            pltpu.SemaphoreType.DMA((4, 4)),
        ],
        compiler_params=pltpu.CompilerParams(vmem_limit_bytes=48 << 20),
        cost_estimate=pl.CostEstimate(
            flops=2 * 1024 * 1024 * 256 * ND, bytes_accessed=6 << 20, transcendentals=0
        ),
        name="convolve",
    )(idx, *xs, *ks)


def errors_kernel(keep_ref, recv_ref, t_ref, e_ref, head_ref, est_ref):
    for h in range(2):
        lanes = slice(h * 128, (h + 1) * 128)
        est_ref[h] = keep_ref[:, lanes] + recv_ref[:, lanes]
        for i in range(SLOTS):
            e = t_ref[i, :, lanes].astype(F32) - est_ref[h, pl.ds(i, TAU, stride=SLOTS), :]
            e_ref[i, :, lanes] = e
            head_ref[i, :, lanes] = e[: LAGS // R]


def make_errors(keep, recv, tgt):
    half = TAU * SLOTS
    return pl.pallas_call(
        errors_kernel,
        out_shape=(
            jax.ShapeDtypeStruct((SLOTS, TAU, RJ), F32),
            jax.ShapeDtypeStruct((SLOTS, LAGS // R, RJ), F32),
        ),
        in_specs=[vmem_spec()] * 3,
        out_specs=(vmem_spec(), vmem_spec()),
        scratch_shapes=[VMEM((2, half, 128), F32)],
        name="make_errors",
    )(keep, recv, tgt)


def corr_kernel(idx, e_ref, head_ref, o_ref, ext_ref, d_ref, sh_ref):
    c = idx[1]
    n = LAGS // R
    last = c == NC - 1
    for i in range(SLOTS):
        ext_ref[i, :TAU, :] = e_ref[i]
        same = head_ref[i]
        if i % NX < NX - 1:
            after = head_ref[i + 1]
        else:
            after = jnp.zeros_like(same)
        ext_ref[i, TAU:, :] = jnp.where(last, after, same)
    past = jnp.transpose(e_ref[...].reshape(SLOTS * TAU, RJ))
    past_hi = past.astype(BF16)
    past_lo = (past - past_hi.astype(F32)).astype(BF16)
    row = lax.broadcasted_iota(jnp.int32, (RJ, RJ), 0)
    col = lax.broadcasted_iota(jnp.int32, (RJ, RJ), 1)
    same_mode = row % J == col % J
    d_ref[...] = jnp.zeros_like(d_ref)
    for a in range(n + 1):
        fut = ext_ref[:, a : a + TAU, :].reshape(SLOTS * TAU, RJ)
        hi = fut.astype(BF16)
        lo = (fut - hi.astype(F32)).astype(BF16)
        gram = (
            jnp.dot(past_hi, hi, preferred_element_type=F32)
            + jnp.dot(past_hi, lo, preferred_element_type=F32)
            + jnp.dot(past_lo, hi, preferred_element_type=F32)
        )
        gram = jnp.where(same_mode, gram, 0.0)
        for p in range(R):
            d_ref[p, a : a + 1, :] = jnp.sum(gram[p * J : (p + 1) * J], axis=0, keepdims=True)
    lane = lax.broadcasted_iota(jnp.int32, (16, RJ), 1)
    here = jnp.zeros((16, RJ), F32)
    before = jnp.zeros((16, RJ), F32)
    for p in range(R):
        v = d_ref[p]
        if p:
            v = pltpu.roll(v, RJ - J * p, 1)
        stays = lane < RJ - J * p
        here = here + jnp.where(stays, v, 0.0)
        before = before + jnp.where(stays, 0.0, v)
    sh_ref[0:16, :] = before
    sh_ref[16:24, :] = jnp.zeros((8, RJ), F32)
    o_ref[...] = here + sh_ref[1:17, :]


def lag_sums(idx, e, head):
    return pl.pallas_call(
        corr_kernel,
        out_shape=jax.ShapeDtypeStruct((16, RJ), F32),
        in_specs=[smem_spec(), vmem_spec(), vmem_spec()],
        out_specs=vmem_spec(),
        scratch_shapes=[
            VMEM((SLOTS, TAU + LAGS // R, RJ), F32),
            VMEM((R, 16, RJ), F32),
            VMEM((24, RJ), F32),
        ],
        name="lag_sums",
    )(idx, e, head)


def finish_kernel(count, r_ref, e_ref, w_ref, f_ref):
    rows = TAU + 16
    group = lane_groups((rows, 128))
    for y in range(NY):
        for q in range(2):
            blocks = [r_ref[y * NX + x, :, q * 128 : (q + 1) * 128] for x in range(NX)]
            for i, v in enumerate(regroup(blocks, group)):
                f_ref[y, pl.ds(4 * q + i, rows, stride=R), :] = v
        lanes = slice(y * 128, (y + 1) * 128)
        e_ref[0, :, lanes] = f_ref[y, 0:TB, :].astype(BF16)
        total0 = f_ref[y, TB : TB + 1, :]
        sums = f_ref[y, TB + 1 : TB + 1 + LAGS, :]
        w_ref[:, lanes] = math.sqrt(count) * (sums / count) / (total0 / count + EPS)


def finish(r, count):
    rows = (TAU + 16) * R
    return pl.pallas_call(
        functools.partial(finish_kernel, count),
        out_shape=(
            jax.ShapeDtypeStruct((1, TB, 512), BF16),
            jax.ShapeDtypeStruct((LAGS, 512), F32),
        ),
        in_specs=[vmem_spec()],
        out_specs=(vmem_spec(), vmem_spec()),
        scratch_shapes=[VMEM((NY, rows, 128), F32)],
        name="finish",
    )(r)


def shift_by(v, axis, by):
    n = lax.axis_size(axis)
    return lax.ppermute(v, axis, [(i, (i + by) % n) for i in range(n)])


def gather_ring(v, axis):
    one = shift_by(v, axis, 1)
    three = shift_by(v, axis, -1)
    two = shift_by(v, axis, 2)
    return [v, one, two, three]


def shards(sensors, kernel, target):
    x, c, z, y = (lax.axis_index(a) for a in ("x", "c", "z", "y"))
    idx = jnp.stack([x, c, z, y]).astype(jnp.int32)
    count = float(16 * 2048)

    own, oth = prep_sensors(idx, sensors)
    got = shift_by(oth, "c", 1)
    pieces = prep_kernel(idx, kernel)
    block = jnp.where(c == 0, jnp.concatenate([own, got]), jnp.concatenate([got, own]))
    row = jnp.stack(gather_ring(block, "x"))
    mine = lax.all_to_all(pieces, "y", 0, 0)
    xs = gather_ring(row, "y")
    ks = gather_ring(mine, "z")
    tgt = lax.all_to_all(prep_target(target), ("y", "x"), 0, 0)
    keep, send = main(idx, xs, ks)
    recv = shift_by(send, "c", 1)
    e, head = make_errors(keep, recv, tgt)
    next_head = shift_by(head, "c", 1)
    sums = lag_sums(idx, e, next_head)
    sums = jnp.sum(lax.all_to_all(jnp.stack([sums] * 8), ("z", "c"), 0, 0), axis=0)
    out = jnp.concatenate([e, jnp.stack([sums] * SLOTS)], axis=1)
    out = lax.all_to_all(out, ("y", "x"), 0, 0)
    return finish(out, count)


def solution(mesh):
    split = Mesh(mesh.devices.reshape(NX, NC, NZ, NY), ("x", "c", "z", "y"))
    member, tm = ("z", "y"), ("x", "c")
    in_specs = (P(member, tm, None), P(member, None, None), P(member, tm, None))
    out_specs = (P(member, tm, None), P())
    return jax.shard_map(shards, mesh=split, in_specs=in_specs, out_specs=out_specs, check_vma=False)
```

```python
import functools
import math

import jax
import jax.numpy as jnp
from jax import lax
from jax.experimental import pallas as pl
from jax.experimental.pallas import tpu as pltpu
from jax.sharding import Mesh
from jax.sharding import PartitionSpec as P

LAGS = 64
EPS = 1e-06

NX, NC, NZ, NY = 4, 2, 4, 4
R = 8
J = 32
RJ = R * J
CH = 128
TB = 256
TAU = TB // R
SLOTS = 16
ZL = 64
ND = ZL // R + 1
KW = 128 + ND * RJ
PX = R * CH
G = 16
ROWS = 256
XROWS = 3 * ROWS


F32 = jnp.float32
BF16 = jnp.bfloat16
VMEM = pltpu.VMEM
ANY = pl.ANY


def smem_spec():
    return pl.BlockSpec(memory_space=pltpu.SMEM)


def vmem_spec():
    return pl.BlockSpec(memory_space=pltpu.VMEM)


def prep_sensors_kernel(idx, s_ref, own_ref, oth_ref, f_ref):
    c = idx[1]
    f_ref[0] = s_ref[0, :, :CH].astype(F32)
    f_ref[1] = s_ref[0, :, CH:].astype(F32)
    for p in range(R):
        lo = f_ref[0, pl.ds(p, TAU, stride=R), :]
        hi = f_ref[1, pl.ds(p, TAU, stride=R), :]
        first = c == 0
        own_ref[:, p * CH : (p + 1) * CH] = jnp.where(first, lo, hi).astype(BF16)
        oth_ref[:, p * CH : (p + 1) * CH] = jnp.where(first, hi, lo).astype(BF16)


def prep_sensors(idx, s):
    return pl.pallas_call(
        prep_sensors_kernel,
        out_shape=(jax.ShapeDtypeStruct((TAU, PX), BF16),) * 2,
        in_specs=[smem_spec(), vmem_spec()],
        out_specs=(vmem_spec(), vmem_spec()),
        scratch_shapes=[VMEM((2, TB, CH), F32)],
        name="prep_sensors",
    )(idx, s)


def prep_kernel_kernel(idx, k_ref, o_ref):
    x = idx[0]
    group = lane_groups((CH, 128))
    for y in range(NY):
        out = None
        for i in range(4):
            v = pltpu.roll(k_ref[i, :, y * 128 : (y + 1) * 128], ((i - x) & 3) * J, 1)
            out = v if out is None else jnp.where(group == i, v, out)
        o_ref[y] = out


def prep_kernel(idx, k):
    return pl.pallas_call(
        prep_kernel_kernel,
        out_shape=jax.ShapeDtypeStruct((NY, CH, 16 * J), BF16),
        grid_spec=pltpu.PrefetchScalarGridSpec(
            num_scalar_prefetch=1,
            grid=(4,),
            in_specs=[pl.BlockSpec((4, CH, 512), lambda q, idx: (q, idx[1], 0))],
            out_specs=pl.BlockSpec((NY, CH, 128), lambda q, idx: (0, 0, q)),
        ),
        name="prep_kernel",
    )(idx, k)


def lane_groups(shape):
    return lax.broadcasted_iota(jnp.int32, shape, len(shape) - 1) // J


def regroup(blocks, group):
    out = []
    for a in range(4):
        acc = None
        for g in range(4):
            shift = (g - a) * J % 128
            v = blocks[g] if shift == 0 else pltpu.roll(blocks[g], shift, 1)
            acc = v if acc is None else jnp.where(group == g, v, acc)
        out.append(acc)
    return out


def prep_target_kernel(t_ref, o_ref, f_ref):
    for y in range(NY):
        f_ref[...] = t_ref[0, :, y * 128 : (y + 1) * 128].astype(F32)
        group = lane_groups((TAU, 128))
        for q in range(2):
            rows = [f_ref[pl.ds(4 * q + i, TAU, stride=R), :] for i in range(4)]
            for x, v in enumerate(regroup(rows, group)):
                o_ref[y * NX + x, :, q * 128 : (q + 1) * 128] = v.astype(BF16)


def prep_target(t):
    return pl.pallas_call(
        prep_target_kernel,
        out_shape=jax.ShapeDtypeStruct((SLOTS, TAU, RJ), BF16),
        in_specs=[vmem_spec()],
        out_specs=vmem_spec(),
        scratch_shapes=[VMEM((TB, 128), F32)],
        name="prep_target",
    )(t)


def expand_rows_kernel(idx, x_ref, o_ref, p_ref):
    x = idx[0]
    row = lax.broadcasted_iota(jnp.int32, (XROWS, 1), 0)
    back = 2 - row // ROWS
    step = (row // G) % 16
    g = row % G
    hi = ((x - (g // 2) % 4) & 3) * 4 + (g // 8) * 2 + g % 2 - back
    src = ((x - (hi >> 2)) & 3) * 64 + ((hi >> 1) & 1) * 32 + (hi & 1) * 16 + step
    src = jnp.where(hi >= 0, src, -1)
    col = lax.broadcasted_iota(jnp.int32, (XROWS, ROWS), 1)
    pick = jnp.where(src == col, 1.0, 0.0).astype(BF16)
    p_ref[...] = pick
    apply_rows(pick, x_ref[...].reshape(ROWS, PX), o_ref)


def apply_rows(pick, v, o_ref):
    for b in range(PX // RJ):
        lanes = slice(b * RJ, (b + 1) * RJ)
        o_ref[:, lanes] = jnp.dot(pick, v[:, lanes], preferred_element_type=F32).astype(BF16)


def more_rows_kernel(p_ref, *refs):
    n = len(refs) // 2
    for x_ref, o_ref in zip(refs[:n], refs[n:]):
        apply_rows(p_ref[...], x_ref[...].reshape(ROWS, PX), o_ref)


def expand_rows(idx, v):
    return pl.pallas_call(
        expand_rows_kernel,
        out_shape=(
            jax.ShapeDtypeStruct((XROWS, PX), BF16),
            jax.ShapeDtypeStruct((XROWS, ROWS), BF16),
        ),
        in_specs=[smem_spec(), vmem_spec()],
        out_specs=(vmem_spec(), vmem_spec()),
        compiler_params=small_params(),
        cost_estimate=cost(1 << 9),
        name="expand_rows",
    )(idx, v)


def more_rows(pick, *vs):
    return pl.pallas_call(
        more_rows_kernel,
        out_shape=(jax.ShapeDtypeStruct((XROWS, PX), BF16),) * len(vs),
        in_specs=[vmem_spec()] * (1 + len(vs)),
        out_specs=(vmem_spec(),) * len(vs),
        compiler_params=small_params(),
        cost_estimate=cost(len(vs) << 9),
        name="more_rows",
    )(pick, *vs)


def small_params():
    return pltpu.CompilerParams(vmem_limit_bytes=24 << 20)


def cost(kflop):
    return pl.CostEstimate(flops=kflop * 1000000, bytes_accessed=1 << 20, transcendentals=0)


def shift_lags_kernel(*refs):
    n = len(refs) // 2
    lane = lax.broadcasted_iota(jnp.int32, (CH, 128), 1)
    zero = jnp.zeros((CH, 128), BF16)
    for k_ref, o_ref in zip(refs[:n], refs[n:]):
        for s in range(4):
            rows = slice(s * CH, (s + 1) * CH)
            prior = zero
            for b in range(KW // 128):
                if 1 <= b <= 16:
                    q = b - 1
                    v = k_ref[q // 4, :, (q % 4) * 128 : (q % 4 + 1) * 128]
                    if s:
                        v = pltpu.roll(v, J * s, 1)
                else:
                    v = zero
                o_ref[rows, b * 128 : (b + 1) * 128] = jnp.where(lane < J * s, prior, v) if s else v
                prior = v


def shift_lags(*ks):
    return pl.pallas_call(
        shift_lags_kernel,
        out_shape=(jax.ShapeDtypeStruct((4 * CH, KW), BF16),) * len(ks),
        in_specs=[vmem_spec()] * len(ks),
        out_specs=(vmem_spec(),) * len(ks),
        compiler_params=small_params(),
        cost_estimate=cost(len(ks) << 9),
        name="shift_lags",
    )(*ks)


def accumulate(idx, acc_ref, first, x_refs, k_ref, dist):
    zs = (idx[2] - dist) & 3
    n = len(x_refs)
    at_rows = slice(first * ROWS, (first + n) * ROWS)

    def step(d, _):
        r0 = pl.multiple_of((32 - 8 * zs - d) * G, G)
        at = pl.multiple_of(d * RJ, 128)
        lo = [r[pl.ds(r0, ROWS), : PX // 2] for r in x_refs]
        hi = [r[pl.ds(r0, ROWS), PX // 2 :] for r in x_refs]
        lo = lo[0] if n == 1 else jnp.concatenate(lo, axis=0)
        hi = hi[0] if n == 1 else jnp.concatenate(hi, axis=0)
        acc_ref[at_rows, :] += jnp.dot(
            lo, k_ref[:, pl.ds(at + 128, RJ)], preferred_element_type=F32
        ) + jnp.dot(hi, k_ref[:, pl.ds(at, RJ)], preferred_element_type=F32)
        return 0

    lax.fori_loop(0, ND, step, 0)


def stage0_kernel(idx, x0, k0, acc_ref):
    acc_ref[...] = jnp.zeros_like(acc_ref)
    accumulate(idx, acc_ref, 0, [x0], k0, 0)


def stage1_kernel(idx, a_ref, x0, x1, x3, k0, k1, k3, acc_ref):
    acc_ref[:ROWS] = a_ref[...]
    acc_ref[ROWS:] = jnp.zeros((2 * ROWS, RJ), F32)
    accumulate(idx, acc_ref, 1, [x1, x3], k0, 0)
    accumulate(idx, acc_ref, 0, [x0, x1, x3], k1, 1)
    accumulate(idx, acc_ref, 0, [x0, x1, x3], k3, 3)


def stage2_kernel(idx, a_ref, x0, x1, x3, x2, k0, k1, k3, k2, keep_ref, send_ref, acc_ref):
    c = idx[1]
    acc_ref[: 3 * ROWS] = a_ref[...]
    acc_ref[3 * ROWS :] = jnp.zeros((ROWS, RJ), F32)
    for k, dist in ((k0, 0), (k1, 1), (k3, 3)):
        accumulate(idx, acc_ref, 3, [x2], k, dist)
    accumulate(idx, acc_ref, 0, [x0, x1, x3, x2], k2, 2)
    for i in range(NY * 16):
        rows = slice(i * 8, (i + 1) * 8)
        keep_ref[rows] = acc_ref[pl.ds(pl.multiple_of(i * G + c * 8, 8), 8), :]
        send_ref[rows] = acc_ref[pl.ds(pl.multiple_of(i * G + 8 - c * 8, 8), 8), :]


def stage(kernel, outs, units, idx, *args, scratch=()):
    return pl.pallas_call(
        kernel,
        out_shape=outs,
        in_specs=[smem_spec()] + [vmem_spec()] * len(args),
        out_specs=jax.tree.map(lambda _: vmem_spec(), outs),
        scratch_shapes=scratch,
        compiler_params=pltpu.CompilerParams(vmem_limit_bytes=32 << 20),
        cost_estimate=cost(units * 2400),
        name=kernel.__name__[:6],
    )(idx, *args)


ORDER = (0, 1, 3, 2)


def errors_kernel(idx, keep_ref, recv_ref, t_ref, e_ref, b_ref, head_ref, est_ref):
    x, y = idx[0], idx[3]
    for w in range(2):
        lanes = slice(w * 128, (w + 1) * 128)
        est_ref[w] = keep_ref[:, lanes] + recv_ref[:, lanes]
    for i, d in enumerate(ORDER):
        for e in range(NX):
            slot = ((y - d) & 3) * NX + ((x - e) & 3)
            for w in range(2):
                lanes = slice(w * 128, (w + 1) * 128)
                est = jnp.concatenate(
                    [est_ref[w, pl.ds(i * 128 + e * 2 + h, 16, stride=8), :] for h in range(2)], axis=0
                )
                v = t_ref[slot, :, lanes].astype(F32) - est
                e_ref[i * NX + e, :, lanes] = v
                b_ref[slot, :, lanes] = v.astype(BF16)
                head_ref[i * NX + e, :, lanes] = v[: LAGS // R]


def make_errors(idx, keep, recv, tgt):
    return pl.pallas_call(
        errors_kernel,
        out_shape=(
            jax.ShapeDtypeStruct((SLOTS, TAU, RJ), F32),
            jax.ShapeDtypeStruct((SLOTS, TAU, RJ), BF16),
            jax.ShapeDtypeStruct((SLOTS, LAGS // R, RJ), F32),
        ),
        in_specs=[smem_spec()] + [vmem_spec()] * 3,
        out_specs=(vmem_spec(),) * 3,
        scratch_shapes=[VMEM((2, TAU * SLOTS, 128), F32)],
        compiler_params=small_params(),
        name="make_errors",
    )(idx, keep, recv, tgt)


def corr_kernel(idx, e_ref, head_ref, o_ref, ext_ref, d_ref, sh_ref):
    x, c = idx[0], idx[1]
    n = LAGS // R
    last = c == NC - 1
    for i in range(SLOTS):
        e = i % NX
        ext_ref[i, :TAU, :] = e_ref[i]
        after = head_ref[i - e + (e - 1) % NX]
        after = jnp.where(((x - e) & 3) == NX - 1, 0.0, after)
        ext_ref[i, TAU:, :] = jnp.where(last, after, head_ref[i])
    past = jnp.transpose(e_ref[...].reshape(SLOTS * TAU, RJ))
    past_hi = past.astype(BF16)
    past_lo = (past - past_hi.astype(F32)).astype(BF16)
    row = lax.broadcasted_iota(jnp.int32, (RJ, RJ), 0)
    col = lax.broadcasted_iota(jnp.int32, (RJ, RJ), 1)
    same_mode = row % J == col % J
    d_ref[...] = jnp.zeros_like(d_ref)
    for a in range(n + 1):
        fut = ext_ref[:, a : a + TAU, :].reshape(SLOTS * TAU, RJ)
        hi = fut.astype(BF16)
        lo = (fut - hi.astype(F32)).astype(BF16)
        gram = (
            jnp.dot(past_hi, hi, preferred_element_type=F32)
            + jnp.dot(past_hi, lo, preferred_element_type=F32)
            + jnp.dot(past_lo, hi, preferred_element_type=F32)
        )
        gram = jnp.where(same_mode, gram, 0.0)
        for p in range(R):
            d_ref[p, a : a + 1, :] = jnp.sum(gram[p * J : (p + 1) * J], axis=0, keepdims=True)
    lane = lax.broadcasted_iota(jnp.int32, (16, RJ), 1)
    here = jnp.zeros((16, RJ), F32)
    before = jnp.zeros((16, RJ), F32)
    for p in range(R):
        v = d_ref[p]
        if p:
            v = pltpu.roll(v, RJ - J * p, 1)
        stays = lane < RJ - J * p
        here = here + jnp.where(stays, v, 0.0)
        before = before + jnp.where(stays, 0.0, v)
    sh_ref[0:16, :] = before
    sh_ref[16:24, :] = jnp.zeros((8, RJ), F32)
    o_ref[...] = here + sh_ref[1:17, :]


def lag_sums(idx, e, head):
    return pl.pallas_call(
        corr_kernel,
        out_shape=jax.ShapeDtypeStruct((16, RJ), F32),
        in_specs=[smem_spec(), vmem_spec(), vmem_spec()],
        out_specs=vmem_spec(),
        scratch_shapes=[
            VMEM((SLOTS, TAU + LAGS // R, RJ), F32),
            VMEM((R, 16, RJ), F32),
            VMEM((24, RJ), F32),
        ],
        name="lag_sums",
    )(idx, e, head)


def pack_kernel(s_ref, b_ref, o_ref, t_ref):
    total = s_ref[0]
    for i in range(1, NZ * NC):
        total = total + s_ref[i]
    hi = total.astype(BF16).astype(F32)
    rest = total - hi
    mid = rest.astype(BF16).astype(F32)
    lo = rest - mid
    t_ref[0:10] = hi[0:10]
    t_ref[10:20] = mid[0:10]
    t_ref[20:30] = lo[0:10]
    t_ref[30:32] = jnp.zeros((2, RJ), F32)
    terms = t_ref[...].astype(BF16)
    for i in range(SLOTS):
        o_ref[i, :TAU] = b_ref[i]
        o_ref[i, TAU:] = terms


def pack(sums, errs):
    return pl.pallas_call(
        pack_kernel,
        out_shape=jax.ShapeDtypeStruct((SLOTS, 2 * TAU, RJ), BF16),
        in_specs=[vmem_spec()] * 2,
        out_specs=vmem_spec(),
        scratch_shapes=[VMEM((32, RJ), F32)],
        compiler_params=small_params(),
        name="pack",
    )(sums, errs)


def finish_kernel(count, r_ref, e_ref, w_ref, f_ref, t_ref):
    for y in range(NY):
        for q in range(2):
            lanes = slice(q * 128, (q + 1) * 128)
            blocks = []
            for x in range(NX):
                v = r_ref[y * NX + x, :, lanes].astype(F32)
                t_ref[...] = v[TAU:]
                sums = t_ref[0:10] + t_ref[10:20] + t_ref[20:30]
                t_ref[0:10] = sums
                blocks.append((v[:TAU], t_ref[0:16]))
            for rows, at, part in ((TAU, 0, 0), (16, TB, 1)):
                group = lane_groups((rows, 128))
                for i, v in enumerate(regroup([b[part] for b in blocks], group)):
                    f_ref[y, pl.ds(at + 4 * q + i, rows, stride=R), :] = v
        lanes = slice(y * 128, (y + 1) * 128)
        e_ref[0, :, lanes] = f_ref[y, 0:TB, :].astype(BF16)
        total0 = f_ref[y, TB : TB + 1, :]
        sums = f_ref[y, TB + 1 : TB + 1 + LAGS, :]
        w_ref[:, lanes] = math.sqrt(count) * (sums / count) / (total0 / count + EPS)


def finish(r, count):
    rows = (TAU + 16) * R
    return pl.pallas_call(
        functools.partial(finish_kernel, count),
        out_shape=(
            jax.ShapeDtypeStruct((1, TB, 512), BF16),
            jax.ShapeDtypeStruct((LAGS, 512), F32),
        ),
        in_specs=[vmem_spec()],
        out_specs=(vmem_spec(), vmem_spec()),
        scratch_shapes=[VMEM((NY, rows, 128), F32), VMEM((32, 128), F32)],
        compiler_params=small_params(),
        name="finish",
    )(r)


def shift_by(v, axis, by):
    n = lax.axis_size(axis)
    return lax.ppermute(v, axis, [(i, (i + by) % n) for i in range(n)])


def gather_ring(v, axis):
    one = shift_by(v, axis, 1)
    three = shift_by(v, axis, -1)
    two = shift_by(v, axis, 2)
    return [v, one, two, three]


def shards(sensors, kernel, target):
    x, c, z, y = (lax.axis_index(a) for a in ("x", "c", "z", "y"))
    idx = jnp.stack([x, c, z, y]).astype(jnp.int32)
    count = float(16 * 2048)

    own, oth = prep_sensors(idx, sensors)
    got = shift_by(oth, "c", 1)
    pieces = prep_kernel(idx, kernel)
    block = jnp.where(c == 0, jnp.concatenate([own, got]), jnp.concatenate([got, own]))
    row = jnp.stack(gather_ring(block, "x"))
    mine = lax.all_to_all(pieces, "y", 0, 0)
    xs = gather_ring(row, "y")
    ks = gather_ring(mine, "z")
    tgt = lax.all_to_all(prep_target(target), ("y", "x"), 0, 0)

    x0, pick = expand_rows(idx, xs[0])
    (k0,) = shift_lags(ks[0])
    acc = stage(stage0_kernel, jax.ShapeDtypeStruct((ROWS, RJ), F32), 1, idx, x0, k0)
    x1, x3 = more_rows(pick, xs[1], xs[3])
    k1, k3 = shift_lags(ks[1], ks[3])
    acc, tgt, x1 = lax.optimization_barrier((acc, tgt, x1))
    acc = stage(
        stage1_kernel, jax.ShapeDtypeStruct((3 * ROWS, RJ), F32), 8, idx, acc, x0, x1, x3, k0, k1, k3
    )
    (x2,) = more_rows(pick, xs[2])
    (k2,) = shift_lags(ks[2])
    half = jax.ShapeDtypeStruct((2 * ROWS, RJ), F32)
    keep, send = stage(
        stage2_kernel,
        (half, half),
        7,
        idx,
        acc,
        x0,
        x1,
        x3,
        x2,
        k0,
        k1,
        k3,
        k2,
        scratch=[VMEM((4 * ROWS, RJ), F32)],
    )
    recv = shift_by(send, "c", 1)
    e, errs, head = make_errors(idx, keep, recv, tgt)
    next_head = shift_by(head, "c", 1)
    sums = lag_sums(idx, e, next_head)
    sums = lax.all_to_all(jnp.stack([sums] * (NZ * NC)), ("z", "c"), 0, 0)
    out = lax.all_to_all(pack(sums, errs), ("y", "x"), 0, 0)
    return finish(out, count)


def solution(mesh):
    split = Mesh(mesh.devices.reshape(NX, NC, NZ, NY), ("x", "c", "z", "y"))
    member, tm = ("z", "y"), ("x", "c")
    in_specs = (P(member, tm, None), P(member, None, None), P(member, tm, None))
    out_specs = (P(member, tm, None), P())
    return jax.shard_map(shards, mesh=split, in_specs=in_specs, out_specs=out_specs, check_vma=False)
```

```python
import functools
import math

import jax
import jax.numpy as jnp
from jax import lax
from jax.experimental import pallas as pl
from jax.experimental.pallas import tpu as pltpu
from jax.sharding import Mesh
from jax.sharding import PartitionSpec as P

LAGS = 64
EPS = 1e-06

NX, NC, NZ, NY = 4, 2, 4, 4
R = 8
J = 32
RJ = R * J
CH = 128
TB = 256
TAU = TB // R
SLOTS = 16
ZL = 64
ND = ZL // R + 1
KW = 128 + ND * RJ
PX = R * CH
G = 16
ROWS = 256
XROWS = 3 * ROWS


F32 = jnp.float32
BF16 = jnp.bfloat16
VMEM = pltpu.VMEM
ANY = pl.ANY


def small_params():
    return pltpu.CompilerParams(vmem_limit_bytes=12 << 20)


def smem_spec():
    return pl.BlockSpec(memory_space=pltpu.SMEM)


def vmem_spec():
    return pl.BlockSpec(memory_space=pltpu.VMEM)


def prep_sensors_kernel(idx, s_ref, own_ref, oth_ref, f_ref):
    c = idx[1]
    f_ref[0] = s_ref[0, :, :CH].astype(F32)
    f_ref[1] = s_ref[0, :, CH:].astype(F32)
    for p in range(R):
        lo = f_ref[0, pl.ds(p, TAU, stride=R), :]
        hi = f_ref[1, pl.ds(p, TAU, stride=R), :]
        first = c == 0
        own_ref[:, p * CH : (p + 1) * CH] = jnp.where(first, lo, hi).astype(BF16)
        oth_ref[:, p * CH : (p + 1) * CH] = jnp.where(first, hi, lo).astype(BF16)


def prep_sensors(idx, s):
    return pl.pallas_call(
        prep_sensors_kernel,
        out_shape=(jax.ShapeDtypeStruct((TAU, PX), BF16),) * 2,
        in_specs=[smem_spec(), vmem_spec()],
        out_specs=(vmem_spec(), vmem_spec()),
        scratch_shapes=[VMEM((2, TB, CH), F32)],
        compiler_params=small_params(),
        name="prep_sensors",
    )(idx, s)


def prep_kernel_kernel(idx, k_ref, o_ref, b_ref, sem):
    x = idx[0]
    rows = pl.ds(pl.multiple_of(idx[1] * CH, CH), CH)
    copies = [
        pltpu.make_async_copy(
            k_ref.at[pl.ds(4 * q, 4), rows, :], b_ref.at[pl.ds(4 * q, 4)], sem.at[q]
        )
        for q in range(4)
    ]
    for cp in copies:
        cp.start()
    group = lane_groups((CH, 128))
    for q in range(4):
        copies[q].wait()
        for y in range(NY):
            out = None
            for i in range(4):
                v = b_ref[4 * q + i, :, y * 128 : (y + 1) * 128]
                v = pltpu.roll(v, ((i - x) & 3) * J, 1)
                out = v if out is None else jnp.where(group == i, v, out)
            o_ref[y, :, q * 128 : (q + 1) * 128] = out


def prep_kernel(idx, k):
    return pl.pallas_call(
        prep_kernel_kernel,
        out_shape=jax.ShapeDtypeStruct((NY, CH, 16 * J), BF16),
        in_specs=[smem_spec(), pl.BlockSpec(memory_space=pltpu.HBM)],
        out_specs=vmem_spec(),
        scratch_shapes=[VMEM((16, CH, 512), BF16), pltpu.SemaphoreType.DMA((4,))],
        compiler_params=small_params(),
        cost_estimate=cost(1 << 9),
        name="prep_kernel",
    )(idx, k)


def lane_groups(shape):
    return lax.broadcasted_iota(jnp.int32, shape, len(shape) - 1) // J


def regroup(blocks, group):
    out = []
    for a in range(4):
        acc = None
        for g in range(4):
            shift = (g - a) * J % 128
            v = blocks[g] if shift == 0 else pltpu.roll(blocks[g], shift, 1)
            acc = v if acc is None else jnp.where(group == g, v, acc)
        out.append(acc)
    return out


def prep_target_kernel(t_ref, o_ref, f_ref):
    for y in range(NY):
        f_ref[...] = t_ref[0, :, y * 128 : (y + 1) * 128].astype(F32)
        group = lane_groups((TAU, 128))
        for q in range(2):
            rows = [f_ref[pl.ds(4 * q + i, TAU, stride=R), :] for i in range(4)]
            for x, v in enumerate(regroup(rows, group)):
                o_ref[y * NX + x, :, q * 128 : (q + 1) * 128] = v.astype(BF16)


def prep_target(t):
    return pl.pallas_call(
        prep_target_kernel,
        out_shape=jax.ShapeDtypeStruct((SLOTS, TAU, RJ), BF16),
        in_specs=[vmem_spec()],
        out_specs=vmem_spec(),
        scratch_shapes=[VMEM((TB, 128), F32)],
        compiler_params=small_params(),
        name="prep_target",
    )(t)


def expand_rows_kernel(idx, *refs):
    a_refs, b_refs, o_refs = refs[:NY], refs[NY : NY + NX], refs[NY + NX :]
    x = idx[0]
    row = lax.broadcasted_iota(jnp.int32, (XROWS, 1), 0)
    back = 2 - row // ROWS
    step = (row // G) % 16
    g = row % G
    hi = ((x - (g // 2) % 4) & 3) * 4 + (g // 8) * 2 + g % 2 - back
    other = ((hi >> 1) + idx[1]) & 1
    src = other * 128 + ((x - (hi >> 2)) & 3) * 32 + (hi & 1) * 16 + step
    src = jnp.where(hi >= 0, src, -1)
    col = lax.broadcasted_iota(jnp.int32, (XROWS, ROWS), 1)
    pick = jnp.where(src == col, 1.0, 0.0).astype(BF16)
    for d in range(NY):
        for b in range(PX // RJ):
            lanes = slice(b * RJ, (b + 1) * RJ)
            v = [a_refs[d][e, :, lanes] for e in range(NX)] + [b_refs[e][d, :, lanes] for e in range(NX)]
            v = jnp.concatenate(v, axis=0)
            o_refs[d][:, lanes] = jnp.dot(pick, v, preferred_element_type=F32).astype(BF16)


def expand_rows(idx, a, b):
    return pl.pallas_call(
        expand_rows_kernel,
        out_shape=(jax.ShapeDtypeStruct((XROWS, PX), BF16),) * NY,
        in_specs=[smem_spec()] + [vmem_spec()] * (NY + NX),
        out_specs=(vmem_spec(),) * NY,
        compiler_params=small_params(),
        cost_estimate=cost(4 << 9),
        name="expand_rows",
    )(idx, *a, *b)


def cost(kflop):
    return pl.CostEstimate(flops=kflop * 1000000, bytes_accessed=1 << 20, transcendentals=0)


def shift_lags_kernel(*refs):
    n = len(refs) // 2
    lane = lax.broadcasted_iota(jnp.int32, (CH, 128), 1)
    zero = jnp.zeros((CH, 128), BF16)
    for k_ref, o_ref in zip(refs[:n], refs[n:]):
        for s in range(4):
            rows = slice(s * CH, (s + 1) * CH)
            prior = zero
            for b in range(KW // 128):
                if 1 <= b <= 16:
                    q = b - 1
                    v = k_ref[q // 4, :, (q % 4) * 128 : (q % 4 + 1) * 128]
                    if s:
                        v = pltpu.roll(v, J * s, 1)
                else:
                    v = zero
                o_ref[rows, b * 128 : (b + 1) * 128] = jnp.where(lane < J * s, prior, v) if s else v
                prior = v


def shift_lags(*ks):
    return pl.pallas_call(
        shift_lags_kernel,
        out_shape=(jax.ShapeDtypeStruct((4 * CH, KW), BF16),) * len(ks),
        in_specs=[vmem_spec()] * len(ks),
        out_specs=(vmem_spec(),) * len(ks),
        compiler_params=small_params(),
        cost_estimate=cost(len(ks) << 9),
        name="shift_lags",
    )(*ks)


def accumulate(idx, acc_ref, x_refs, k_ref, dist):
    zs = (idx[2] - dist) & 3

    def step(g, _):
        lhs, rhs = [], []
        for i in range(3):
            d = 3 * g + i
            r0 = pl.multiple_of((32 - 8 * zs - d) * G, G)
            at = pl.multiple_of(d * RJ, 128)
            lhs.append(jnp.concatenate([r[pl.ds(r0, ROWS), :] for r in x_refs], axis=0))
            rhs += [k_ref[:, pl.ds(at + 128, RJ)], k_ref[:, pl.ds(at, RJ)]]
        acc_ref[...] += jnp.dot(
            jnp.concatenate(lhs, axis=1), jnp.concatenate(rhs, axis=0), preferred_element_type=F32
        )
        return 0

    lax.fori_loop(0, ND // 3, step, 0)


def stage0_kernel(idx, x0, x1, x2, x3, k0, acc_ref):
    acc_ref[...] = jnp.zeros_like(acc_ref)
    accumulate(idx, acc_ref, [x0, x1, x2, x3], k0, 0)


def stage1_kernel(idx, a_ref, x0, x1, x2, x3, k3, k1, acc_ref):
    acc_ref[...] = a_ref[...]
    accumulate(idx, acc_ref, [x0, x1, x2, x3], k3, 3)
    accumulate(idx, acc_ref, [x0, x1, x2, x3], k1, 1)


def stage2_kernel(idx, a_ref, x0, x1, x2, x3, k2, keep_ref, send_ref, acc_ref):
    c = idx[1]
    acc_ref[...] = a_ref[...]
    accumulate(idx, acc_ref, [x0, x1, x2, x3], k2, 2)
    for i in range(NY * 16):
        rows = slice(i * 8, (i + 1) * 8)
        keep_ref[rows] = acc_ref[pl.ds(pl.multiple_of(i * G + c * 8, 8), 8), :]
        send_ref[rows] = acc_ref[pl.ds(pl.multiple_of(i * G + 8 - c * 8, 8), 8), :]


def stage(kernel, outs, units, idx, *args, scratch=()):
    return pl.pallas_call(
        kernel,
        out_shape=outs,
        in_specs=[smem_spec()] + [vmem_spec()] * len(args),
        out_specs=jax.tree.map(lambda _: vmem_spec(), outs),
        scratch_shapes=scratch,
        compiler_params=pltpu.CompilerParams(vmem_limit_bytes=16 << 20),
        cost_estimate=cost(units * 2400),
        name=kernel.__name__[:6],
    )(idx, *args)


def errors_kernel(idx, keep_ref, recv_ref, t_ref, e_ref, b_ref, head_ref, est_ref):
    x, y = idx[0], idx[3]
    for w in range(2):
        lanes = slice(w * 128, (w + 1) * 128)
        est_ref[w] = keep_ref[:, lanes] + recv_ref[:, lanes]
    for d in range(NY):
        for e in range(NX):
            slot = ((y - d) & 3) * NX + ((x - e) & 3)
            for w in range(2):
                lanes = slice(w * 128, (w + 1) * 128)
                est = jnp.concatenate(
                    [est_ref[w, pl.ds(d * 128 + e * 2 + h, 16, stride=8), :] for h in range(2)], axis=0
                )
                v = t_ref[slot, :, lanes].astype(F32) - est
                e_ref[d * NX + e, :, lanes] = v
                b_ref[slot, :, lanes] = v.astype(BF16)
                head_ref[d * NX + e, :, lanes] = v[: LAGS // R]


def make_errors(idx, keep, recv, tgt):
    return pl.pallas_call(
        errors_kernel,
        out_shape=(
            jax.ShapeDtypeStruct((SLOTS, TAU, RJ), F32),
            jax.ShapeDtypeStruct((SLOTS, TAU, RJ), BF16),
            jax.ShapeDtypeStruct((SLOTS, LAGS // R, RJ), F32),
        ),
        in_specs=[smem_spec()] + [vmem_spec()] * 3,
        out_specs=(vmem_spec(),) * 3,
        scratch_shapes=[VMEM((2, TAU * SLOTS, 128), F32)],
        compiler_params=small_params(),
        name="make_errors",
    )(idx, keep, recv, tgt)


def corr_kernel(idx, e_ref, head_ref, o_ref, ext_ref, d_ref, sh_ref):
    x, c = idx[0], idx[1]
    n = LAGS // R
    last = c == NC - 1
    for i in range(SLOTS):
        e = i % NX
        ext_ref[i, :TAU, :] = e_ref[i]
        after = head_ref[i - e + (e - 1) % NX]
        after = jnp.where(((x - e) & 3) == NX - 1, 0.0, after)
        ext_ref[i, TAU:, :] = jnp.where(last, after, head_ref[i])
    past = jnp.transpose(e_ref[...].reshape(SLOTS * TAU, RJ))
    past_hi = past.astype(BF16)
    past_lo = (past - past_hi.astype(F32)).astype(BF16)
    row = lax.broadcasted_iota(jnp.int32, (RJ, RJ), 0)
    col = lax.broadcasted_iota(jnp.int32, (RJ, RJ), 1)
    same_mode = row % J == col % J
    d_ref[...] = jnp.zeros_like(d_ref)
    for a in range(n + 1):
        fut = ext_ref[:, a : a + TAU, :].reshape(SLOTS * TAU, RJ)
        hi = fut.astype(BF16)
        lo = (fut - hi.astype(F32)).astype(BF16)
        gram = (
            jnp.dot(past_hi, hi, preferred_element_type=F32)
            + jnp.dot(past_hi, lo, preferred_element_type=F32)
            + jnp.dot(past_lo, hi, preferred_element_type=F32)
        )
        gram = jnp.where(same_mode, gram, 0.0)
        for p in range(R):
            d_ref[p, a : a + 1, :] = jnp.sum(gram[p * J : (p + 1) * J], axis=0, keepdims=True)
    lane = lax.broadcasted_iota(jnp.int32, (16, RJ), 1)
    here = jnp.zeros((16, RJ), F32)
    before = jnp.zeros((16, RJ), F32)
    for p in range(R):
        v = d_ref[p]
        if p:
            v = pltpu.roll(v, RJ - J * p, 1)
        stays = lane < RJ - J * p
        here = here + jnp.where(stays, v, 0.0)
        before = before + jnp.where(stays, 0.0, v)
    sh_ref[0:16, :] = before
    sh_ref[16:24, :] = jnp.zeros((8, RJ), F32)
    total = here + sh_ref[1:17, :]
    for i in range(NZ * NC):
        o_ref[i] = total


def lag_sums(idx, e, head):
    return pl.pallas_call(
        corr_kernel,
        out_shape=jax.ShapeDtypeStruct((NZ * NC, 16, RJ), F32),
        in_specs=[smem_spec(), vmem_spec(), vmem_spec()],
        out_specs=vmem_spec(),
        scratch_shapes=[
            VMEM((SLOTS, TAU + LAGS // R, RJ), F32),
            VMEM((R, 16, RJ), F32),
            VMEM((24, RJ), F32),
        ],
        compiler_params=small_params(),
        name="lag_sums",
    )(idx, e, head)


def whiten_kernel(count, s_ref, e_ref, o_ref):
    total = s_ref[0]
    for i in range(1, NZ * NC):
        total = total + s_ref[i]
    lane = lax.broadcasted_iota(jnp.int32, (8, RJ), 1)
    base = jnp.where(lane < J, total[:8], 0.0)[0:1]
    zero_lag = base
    for i in range(1, R):
        zero_lag = zero_lag + pltpu.roll(base, i * J, 1)
    moved = pltpu.roll(total, RJ - J, 1)
    sums = jnp.where(lane < RJ - J, moved[0:8], moved[1:9])
    w = math.sqrt(count) * (sums / count) / (zero_lag / count + EPS)
    hi = w.astype(BF16).astype(F32)
    terms = jnp.concatenate([hi, w - hi], axis=0).astype(BF16)
    for i in range(SLOTS):
        o_ref[i, :TAU] = e_ref[i]
        o_ref[i, TAU:] = terms


def whiten(sums, errs, count):
    return pl.pallas_call(
        functools.partial(whiten_kernel, count),
        out_shape=jax.ShapeDtypeStruct((SLOTS, TAU + 16, RJ), BF16),
        in_specs=[vmem_spec()] * 2,
        out_specs=vmem_spec(),
        compiler_params=small_params(),
        name="whiten",
    )(sums, errs)


def unpack_kernel(r_ref, e_ref, w_ref, f_ref):
    for y in range(NY):
        for q in range(2):
            lanes = slice(q * 128, (q + 1) * 128)
            blocks = [r_ref[y * NX + x, :, lanes].astype(F32) for x in range(NX)]
            parts = (
                (0, TAU, [v[:TAU] for v in blocks]),
                (TB, 8, [v[TAU : TAU + 8] + v[TAU + 8 :] for v in blocks]),
            )
            for at, n, v in parts:
                for i, o in enumerate(regroup(v, lane_groups((n, 128)))):
                    f_ref[y, pl.ds(at + 4 * q + i, n, stride=R), :] = o
        e_ref[0, :, y * 128 : (y + 1) * 128] = f_ref[y, :TB].astype(BF16)
        w_ref[:, y * 128 : (y + 1) * 128] = f_ref[y, TB:]


def unpack(r):
    return pl.pallas_call(
        unpack_kernel,
        out_shape=(
            jax.ShapeDtypeStruct((1, TB, 512), BF16),
            jax.ShapeDtypeStruct((LAGS, 512), F32),
        ),
        in_specs=[vmem_spec()],
        out_specs=(vmem_spec(), vmem_spec()),
        scratch_shapes=[VMEM((NY, TB + LAGS, 128), F32)],
        compiler_params=small_params(),
        name="unpack",
    )(r)


def shift_by(v, axis, by):
    n = lax.axis_size(axis)
    return lax.ppermute(v, axis, [(i, (i + by) % n) for i in range(n)])


def gather_ring(v, axis):
    one = shift_by(v, axis, 1)
    three = shift_by(v, axis, -1)
    two = shift_by(v, axis, 2)
    return [v, one, two, three]


def shards(sensors, kernel, target):
    x, c, z, y = (lax.axis_index(a) for a in ("x", "c", "z", "y"))
    idx = jnp.stack([x, c, z, y]).astype(jnp.int32)
    count = float(16 * 2048)

    own, oth = prep_sensors(idx, sensors)
    got = shift_by(oth, "c", 1)
    row = jnp.stack(gather_ring(own, "x"))
    pieces = prep_kernel(idx, kernel)
    mine = lax.all_to_all(pieces, "y", 0, 0)
    target, _ = lax.optimization_barrier((target, pieces))
    column = jnp.stack(gather_ring(got, "y"))
    tgt = lax.all_to_all(prep_target(target), ("y", "x"), 0, 0)
    rows = gather_ring(row, "y")
    columns = gather_ring(column, "x")
    ks = gather_ring(mine, "z")
    rows[0], mine, tgt = lax.optimization_barrier((rows[0], mine, tgt))

    (k0,) = shift_lags(mine)
    xs = expand_rows(idx, rows, columns)
    whole = jax.ShapeDtypeStruct((4 * ROWS, RJ), F32)
    acc = stage(stage0_kernel, whole, 4, idx, *xs, k0)
    k1, k3 = shift_lags(ks[1], ks[3])
    acc = stage(stage1_kernel, whole, 8, idx, acc, *xs, k3, k1)
    (k2,) = shift_lags(ks[2])
    half = jax.ShapeDtypeStruct((2 * ROWS, RJ), F32)
    keep, send = stage(
        stage2_kernel, (half, half), 4, idx, acc, *xs, k2, scratch=[VMEM((4 * ROWS, RJ), F32)]
    )
    recv = shift_by(send, "c", 1)
    e, errs, head = make_errors(idx, keep, recv, tgt)
    next_head = shift_by(head, "c", 1)
    sums = lax.all_to_all(lag_sums(idx, e, next_head), ("z", "c"), 0, 0)
    return unpack(lax.all_to_all(whiten(sums, errs, count), ("y", "x"), 0, 0))


def solution(mesh):
    split = Mesh(mesh.devices.reshape(NX, NC, NZ, NY), ("x", "c", "z", "y"))
    member, tm = ("z", "y"), ("x", "c")
    in_specs = (P(member, tm, None), P(member, None, None), P(member, tm, None))
    out_specs = (P(member, tm, None), P())
    return jax.shard_map(shards, mesh=split, in_specs=in_specs, out_specs=out_specs, check_vma=False)
```

```python
import functools
import math

import jax
import jax.numpy as jnp
from jax import lax
from jax.experimental import pallas as pl
from jax.experimental.pallas import tpu as pltpu
from jax.sharding import Mesh
from jax.sharding import PartitionSpec as P


LAGS = 64
EPS = 1e-06

NX, NC, NZ, NY = 4, 2, 4, 4
R = 8
J = 32
RJ = R * J
CH = 128
TB = 256
TAU = TB // R
SLOTS = 16
ZL = 64
ND = ZL // R + 1
KW = 128 + ND * RJ
PX = R * CH
KP = 16 * J
G = 16
ROWS = 256
XROWS = 3 * ROWS


F32 = jnp.float32
BF16 = jnp.bfloat16
VMEM = pltpu.VMEM
ANY = pl.ANY


def small_params():
    return pltpu.CompilerParams(vmem_limit_bytes=12 << 20)


def smem_spec():
    return pl.BlockSpec(memory_space=pltpu.SMEM)


def vmem_spec():
    return pl.BlockSpec(memory_space=pltpu.VMEM)


def prep_sensors_kernel(idx, s_ref, own_ref, oth_ref, f_ref):
    c = idx[1]
    f_ref[0] = s_ref[0, :, :CH].astype(F32)
    f_ref[1] = s_ref[0, :, CH:].astype(F32)
    for p in range(R):
        lo = f_ref[0, pl.ds(p, TAU, stride=R), :]
        hi = f_ref[1, pl.ds(p, TAU, stride=R), :]
        first = c == 0
        own_ref[:, p * CH : (p + 1) * CH] = jnp.where(first, lo, hi).astype(BF16)
        oth_ref[:, p * CH : (p + 1) * CH] = jnp.where(first, hi, lo).astype(BF16)


def prep_sensors(idx, s):
    return pl.pallas_call(
        prep_sensors_kernel,
        out_shape=(jax.ShapeDtypeStruct((TAU, PX), BF16),) * 2,
        in_specs=[smem_spec(), vmem_spec()],
        out_specs=(vmem_spec(), vmem_spec()),
        scratch_shapes=[VMEM((2, TB, CH), F32)],
        compiler_params=small_params(),
        name="prep_sensors",
    )(idx, s)


def prep_kernel_kernel(idx, k_ref, t_ref, o_ref, b_ref, f_ref, sem):
    x = idx[0]
    rows = pl.ds(pl.multiple_of(idx[1] * CH, CH), CH)
    copies = [
        pltpu.make_async_copy(
            k_ref.at[pl.ds(4 * q, 4), rows, :], b_ref.at[pl.ds(4 * q, 4)], sem.at[q]
        )
        for q in range(4)
    ]
    for cp in copies:
        cp.start()
    group = lane_groups((TAU, 128))
    for y in range(NY):
        f_ref[...] = t_ref[0, :, y * 128 : (y + 1) * 128].astype(F32)
        for q in range(2):
            v = [f_ref[pl.ds(4 * q + i, TAU, stride=R), :] for i in range(4)]
            for i, out in enumerate(regroup(v, group)):
                o_ref[y, i * TAU : (i + 1) * TAU, KP + q * 128 : KP + (q + 1) * 128] = out.astype(BF16)
    group = lane_groups((CH, 128))
    for q in range(4):
        copies[q].wait()
        for y in range(NY):
            out = None
            for i in range(4):
                v = b_ref[4 * q + i, :, y * 128 : (y + 1) * 128]
                v = pltpu.roll(v, ((i - x) & 3) * J, 1)
                out = v if out is None else jnp.where(group == i, v, out)
            o_ref[y, :, q * 128 : (q + 1) * 128] = out


def prep_kernel(idx, k, t):
    return pl.pallas_call(
        prep_kernel_kernel,
        out_shape=jax.ShapeDtypeStruct((NY, CH, KP + RJ), BF16),
        in_specs=[smem_spec(), pl.BlockSpec(memory_space=ANY), vmem_spec()],
        out_specs=vmem_spec(),
        scratch_shapes=[
            VMEM((16, CH, 512), BF16),
            VMEM((TB, 128), F32),
            pltpu.SemaphoreType.DMA((4,)),
        ],
        compiler_params=pltpu.CompilerParams(vmem_limit_bytes=58 << 20),
        cost_estimate=cost(1 << 9),
        name="prep_kernel",
    )(idx, k, t)


def part_kernel(idx, r_ref, k_ref, *t_refs):
    k_ref[...] = r_ref[:, :, :KP]
    for e in range(NX):
        rows = pl.ds(pl.multiple_of(((idx[0] + e) & 3) * TAU, TAU), TAU)
        t_refs[e][...] = r_ref[:, rows, KP:]


def part(idx, r):
    return pl.pallas_call(
        part_kernel,
        out_shape=(jax.ShapeDtypeStruct((NY, CH, KP), BF16),)
        + (jax.ShapeDtypeStruct((NY, TAU, RJ), BF16),) * NX,
        in_specs=[smem_spec(), vmem_spec()],
        out_specs=(vmem_spec(),) * (1 + NX),
        compiler_params=small_params(),
        cost_estimate=cost(1 << 9),
        name="part",
    )(idx, r)


def lane_groups(shape):
    return lax.broadcasted_iota(jnp.int32, shape, len(shape) - 1) // J


def regroup(blocks, group):
    out = []
    for a in range(4):
        acc = None
        for g in range(4):
            shift = (g - a) * J % 128
            v = blocks[g] if shift == 0 else pltpu.roll(blocks[g], shift, 1)
            acc = v if acc is None else jnp.where(group == g, v, acc)
        out.append(acc)
    return out


def expand_rows_kernel(idx, *refs):
    a_refs, b_refs, o_refs = refs[:NY], refs[NY : NY + NX], refs[NY + NX :]
    x = idx[0]
    row = lax.broadcasted_iota(jnp.int32, (XROWS, 1), 0)
    back = 2 - row // ROWS
    step = (row // G) % 16
    g = row % G
    hi = ((x - (g // 2) % 4) & 3) * 4 + (g // 8) * 2 + g % 2 - back
    other = ((hi >> 1) + idx[1]) & 1
    src = other * 128 + ((x - (hi >> 2)) & 3) * 32 + (hi & 1) * 16 + step
    src = jnp.where(hi >= 0, src, -1)
    col = lax.broadcasted_iota(jnp.int32, (XROWS, ROWS), 1)
    pick = jnp.where(src == col, 1.0, 0.0).astype(BF16)
    for d in range(NY):
        for b in range(PX // RJ):
            lanes = slice(b * RJ, (b + 1) * RJ)
            v = [a_refs[d][e, :, lanes] for e in range(NX)]
            v += [b_refs[e][d, :, lanes] for e in range(NX)]
            v = jnp.concatenate(v, axis=0)
            o_refs[d][:, lanes] = jnp.dot(pick, v, preferred_element_type=F32).astype(BF16)


def expand_rows(idx, a, b):
    return pl.pallas_call(
        expand_rows_kernel,
        out_shape=(jax.ShapeDtypeStruct((XROWS, PX), BF16),) * NY,
        in_specs=[smem_spec()] + [vmem_spec()] * (NY + NX),
        out_specs=(vmem_spec(),) * NY,
        compiler_params=small_params(),
        cost_estimate=cost(4 << 9),
        name="expand_rows",
    )(idx, *a, *b)


def cost(kflop):
    return pl.CostEstimate(flops=kflop * 1000000, bytes_accessed=1 << 20, transcendentals=0)


def shift_lags_kernel(*refs):
    n = len(refs) // 2
    lane = lax.broadcasted_iota(jnp.int32, (CH, 128), 1)
    zero = jnp.zeros((CH, 128), BF16)
    for k_ref, o_ref in zip(refs[:n], refs[n:]):
        for s in range(4):
            rows = slice(s * CH, (s + 1) * CH)
            prior = zero
            for b in range(KW // 128):
                if 1 <= b <= 16:
                    q = b - 1
                    v = k_ref[q // 4, :, (q % 4) * 128 : (q % 4 + 1) * 128]
                    if s:
                        v = pltpu.roll(v, J * s, 1)
                else:
                    v = zero
                o_ref[rows, b * 128 : (b + 1) * 128] = jnp.where(lane < J * s, prior, v) if s else v
                prior = v


def shift_lags(*ks):
    return pl.pallas_call(
        shift_lags_kernel,
        out_shape=(jax.ShapeDtypeStruct((4 * CH, KW), BF16),) * len(ks),
        in_specs=[vmem_spec()] * len(ks),
        out_specs=(vmem_spec(),) * len(ks),
        compiler_params=small_params(),
        cost_estimate=cost(len(ks) << 9),
        name="shift_lags",
    )(*ks)


def accumulate(idx, acc_ref, x_refs, k_ref, dist):
    zs = (idx[2] - dist) & 3

    def step(g, _):
        lhs, rhs = [], []
        for i in range(3):
            d = 3 * g + i
            r0 = pl.multiple_of((32 - 8 * zs - d) * G, G)
            at = pl.multiple_of(d * RJ, 128)
            lhs.append(jnp.concatenate([r[pl.ds(r0, ROWS), :] for r in x_refs], axis=0))
            rhs += [k_ref[:, pl.ds(at + 128, RJ)], k_ref[:, pl.ds(at, RJ)]]
        acc_ref[...] += jnp.dot(
            jnp.concatenate(lhs, axis=1), jnp.concatenate(rhs, axis=0), preferred_element_type=F32
        )
        return 0

    lax.fori_loop(0, ND // 3, step, 0)


def stage0_kernel(idx, x0, x1, x2, x3, k0, acc_ref):
    acc_ref[...] = jnp.zeros_like(acc_ref)
    accumulate(idx, acc_ref, [x0, x1, x2, x3], k0, 0)


def stage1_kernel(idx, a_ref, x0, x1, x2, x3, k3, k1, acc_ref):
    acc_ref[...] = a_ref[...]
    accumulate(idx, acc_ref, [x0, x1, x2, x3], k3, 3)
    accumulate(idx, acc_ref, [x0, x1, x2, x3], k1, 1)


def stage2_kernel(idx, a_ref, x0, x1, x2, x3, k2, keep_ref, send_ref, acc_ref):
    c = idx[1]
    acc_ref[...] = a_ref[...]
    accumulate(idx, acc_ref, [x0, x1, x2, x3], k2, 2)
    for i in range(NY * 16):
        rows = slice(i * 8, (i + 1) * 8)
        keep_ref[rows] = acc_ref[pl.ds(pl.multiple_of(i * G + c * 8, 8), 8), :]
        send_ref[rows] = acc_ref[pl.ds(pl.multiple_of(i * G + 8 - c * 8, 8), 8), :]


def stage(kernel, outs, units, idx, *args, scratch=()):
    return pl.pallas_call(
        kernel,
        out_shape=outs,
        in_specs=[smem_spec()] + [vmem_spec()] * len(args),
        out_specs=jax.tree.map(lambda _: vmem_spec(), outs),
        scratch_shapes=scratch,
        compiler_params=pltpu.CompilerParams(vmem_limit_bytes=16 << 20),
        cost_estimate=cost(units * 2400),
    )(idx, *args)


def errors_kernel(idx, keep_ref, recv_ref, t0, t1, t2, t3, e_ref, b_ref, head_ref, est_ref):
    x, y = idx[0], idx[3]
    for w in range(2):
        lanes = slice(w * 128, (w + 1) * 128)
        est_ref[w] = keep_ref[:, lanes] + recv_ref[:, lanes]
    for d in range(NY):
        for e in range(NX):
            slot = ((y - d) & 3) * NX + ((x - e) & 3)
            for w in range(2):
                lanes = slice(w * 128, (w + 1) * 128)
                est = jnp.concatenate(
                    [est_ref[w, pl.ds(d * 128 + e * 2 + h, 16, stride=8), :] for h in range(2)], axis=0
                )
                v = (t0, t1, t2, t3)[e][(y - d) & 3, :, lanes].astype(F32) - est
                e_ref[d * NX + e, :, lanes] = v
                b_ref[slot, :, lanes] = v.astype(BF16)
                head_ref[d * NX + e, :, lanes] = v[: LAGS // R]


def make_errors(idx, keep, recv, *tgt):
    return pl.pallas_call(
        errors_kernel,
        out_shape=(
            jax.ShapeDtypeStruct((SLOTS, TAU, RJ), F32),
            jax.ShapeDtypeStruct((SLOTS, TAU, RJ), BF16),
            jax.ShapeDtypeStruct((SLOTS, LAGS // R, RJ), F32),
        ),
        in_specs=[smem_spec()] + [vmem_spec()] * 6,
        out_specs=(vmem_spec(),) * 3,
        scratch_shapes=[VMEM((2, TAU * SLOTS, 128), F32)],
        compiler_params=small_params(),
        name="make_errors",
    )(idx, keep, recv, *tgt)


def corr_kernel(idx, e_ref, head_ref, o_ref, ext_ref, d_ref, sh_ref):
    x, c = idx[0], idx[1]
    n = LAGS // R
    last = c == NC - 1
    for i in range(SLOTS):
        e = i % NX
        ext_ref[i, :TAU, :] = e_ref[i]
        after = head_ref[i - e + (e - 1) % NX]
        after = jnp.where(((x - e) & 3) == NX - 1, 0.0, after)
        ext_ref[i, TAU:, :] = jnp.where(last, after, head_ref[i])
    past = jnp.transpose(e_ref[...].reshape(SLOTS * TAU, RJ))
    past_hi = past.astype(BF16)
    past_lo = (past - past_hi.astype(F32)).astype(BF16)
    row = lax.broadcasted_iota(jnp.int32, (RJ, RJ), 0)
    col = lax.broadcasted_iota(jnp.int32, (RJ, RJ), 1)
    same_mode = row % J == col % J
    d_ref[...] = jnp.zeros_like(d_ref)
    for a in range(n + 1):
        fut = ext_ref[:, a : a + TAU, :].reshape(SLOTS * TAU, RJ)
        hi = fut.astype(BF16)
        lo = (fut - hi.astype(F32)).astype(BF16)
        gram = (
            jnp.dot(past_hi, hi, preferred_element_type=F32)
            + jnp.dot(past_hi, lo, preferred_element_type=F32)
            + jnp.dot(past_lo, hi, preferred_element_type=F32)
        )
        gram = jnp.where(same_mode, gram, 0.0)
        for p in range(R):
            d_ref[p, a : a + 1, :] = jnp.sum(gram[p * J : (p + 1) * J], axis=0, keepdims=True)
    lane = lax.broadcasted_iota(jnp.int32, (16, RJ), 1)
    here = jnp.zeros((16, RJ), F32)
    before = jnp.zeros((16, RJ), F32)
    for p in range(R):
        v = d_ref[p]
        if p:
            v = pltpu.roll(v, RJ - J * p, 1)
        stays = lane < RJ - J * p
        here = here + jnp.where(stays, v, 0.0)
        before = before + jnp.where(stays, 0.0, v)
    sh_ref[0:16, :] = before
    sh_ref[16:24, :] = jnp.zeros((8, RJ), F32)
    total = here + sh_ref[1:17, :]
    for i in range(NZ * NC):
        o_ref[i] = total


def lag_sums(idx, e, head):
    return pl.pallas_call(
        corr_kernel,
        out_shape=jax.ShapeDtypeStruct((NZ * NC, 16, RJ), F32),
        in_specs=[smem_spec(), vmem_spec(), vmem_spec()],
        out_specs=vmem_spec(),
        scratch_shapes=[
            VMEM((SLOTS, TAU + LAGS // R, RJ), F32),
            VMEM((R, 16, RJ), F32),
            VMEM((24, RJ), F32),
        ],
        compiler_params=small_params(),
        name="lag_sums",
    )(idx, e, head)


def whiten_kernel(count, s_ref, e_ref, o_ref):
    total = s_ref[0]
    for i in range(1, NZ * NC):
        total = total + s_ref[i]
    lane = lax.broadcasted_iota(jnp.int32, (8, RJ), 1)
    base = jnp.where(lane < J, total[:8], 0.0)[0:1]
    zero_lag = base
    for i in range(1, R):
        zero_lag = zero_lag + pltpu.roll(base, i * J, 1)
    moved = pltpu.roll(total, RJ - J, 1)
    sums = jnp.where(lane < RJ - J, moved[0:8], moved[1:9])
    w = math.sqrt(count) * (sums / count) / (zero_lag / count + EPS)
    hi = w.astype(BF16).astype(F32)
    terms = jnp.concatenate([hi, w - hi], axis=0).astype(BF16)
    for i in range(SLOTS):
        o_ref[i, :TAU] = e_ref[i]
        o_ref[i, TAU:] = terms


def whiten(sums, errs, count):
    return pl.pallas_call(
        functools.partial(whiten_kernel, count),
        out_shape=jax.ShapeDtypeStruct((SLOTS, TAU + 16, RJ), BF16),
        in_specs=[vmem_spec()] * 2,
        out_specs=vmem_spec(),
        compiler_params=small_params(),
        name="whiten",
    )(sums, errs)


def unpack_kernel(r_ref, e_ref, w_ref, f_ref):
    for y in range(NY):
        for q in range(2):
            lanes = slice(q * 128, (q + 1) * 128)
            blocks = [r_ref[y * NX + x, :, lanes].astype(F32) for x in range(NX)]
            parts = (
                (0, TAU, [v[:TAU] for v in blocks]),
                (TB, 8, [v[TAU : TAU + 8] + v[TAU + 8 :] for v in blocks]),
            )
            for at, n, v in parts:
                for i, o in enumerate(regroup(v, lane_groups((n, 128)))):
                    f_ref[y, pl.ds(at + 4 * q + i, n, stride=R), :] = o
        e_ref[0, :, y * 128 : (y + 1) * 128] = f_ref[y, :TB].astype(BF16)
        w_ref[:, y * 128 : (y + 1) * 128] = f_ref[y, TB:]


def unpack(r):
    return pl.pallas_call(
        unpack_kernel,
        out_shape=(
            jax.ShapeDtypeStruct((1, TB, 512), BF16),
            jax.ShapeDtypeStruct((LAGS, 512), F32),
        ),
        in_specs=[vmem_spec()],
        out_specs=(vmem_spec(), vmem_spec()),
        scratch_shapes=[VMEM((NY, TB + LAGS, 128), F32)],
        compiler_params=small_params(),
        name="unpack",
    )(r)


def shift_by(v, axis, by):
    n = lax.axis_size(axis)
    return lax.ppermute(v, axis, [(i, (i + by) % n) for i in range(n)])


def gather_ring(v, axis):
    out = [v]
    for by in (1, 2, -1):
        out.append(shift_by(v, axis, by))
    return out


def body(sensors, kernel, target):
    x, c, z, y = (lax.axis_index(a) for a in ("x", "c", "z", "y"))
    idx = jnp.stack([x, c, z, y]).astype(jnp.int32)
    count = float(16 * 2048)

    own, oth = prep_sensors(idx, sensors)
    got = shift_by(oth, "c", 1)
    row = jnp.stack(gather_ring(own, "x"))
    pieces = prep_kernel(idx, kernel, target)
    pieces = lax.all_to_all(pieces, "y", 0, 0)
    column = jnp.stack(gather_ring(got, "y"))
    mine, *tgt = part(idx, pieces)
    rows = gather_ring(row, "y")
    columns = gather_ring(column, "x")
    ks = gather_ring(mine, "z")
    for e in range(1, NX):
        tgt[e] = shift_by(tgt[e], "x", e)

    (k0,) = shift_lags(mine)
    xs = expand_rows(idx, rows, columns)
    whole = jax.ShapeDtypeStruct((4 * ROWS, RJ), F32)
    acc = stage(stage0_kernel, whole, 4, idx, *xs, k0)
    k1, k3 = shift_lags(ks[1], ks[3])
    acc = stage(stage1_kernel, whole, 8, idx, acc, *xs, k3, k1)
    (k2,) = shift_lags(ks[2])
    half = jax.ShapeDtypeStruct((2 * ROWS, RJ), F32)
    keep, send = stage(
        stage2_kernel, (half, half), 4, idx, acc, *xs, k2, scratch=[VMEM((4 * ROWS, RJ), F32)]
    )
    recv = shift_by(send, "c", 1)
    e, errs, head = make_errors(idx, keep, recv, *tgt)
    next_head = shift_by(head, "c", 1)
    sums = lax.all_to_all(lag_sums(idx, e, next_head), ("z", "c"), 0, 0)
    return unpack(lax.all_to_all(whiten(sums, errs, count), ("y", "x"), 0, 0))


def solution(mesh):
    split = Mesh(mesh.devices.reshape(NX, NC, NZ, NY), ("x", "c", "z", "y"))
    member, tm = ("z", "y"), ("x", "c")
    in_specs = (P(member, tm, None), P(member, None, None), P(member, tm, None))
    out_specs = (P(member, tm, None), P())
    return jax.shard_map(body, mesh=split, in_specs=in_specs, out_specs=out_specs, check_vma=False)
```

```python
import functools
import math

import jax
import jax.numpy as jnp
from jax import lax
from jax.experimental import pallas as pl
from jax.experimental.pallas import tpu as pltpu
from jax.sharding import Mesh
from jax.sharding import PartitionSpec as P


LAGS = 64
EPS = 1e-06

NX, NC, NZ, NY = 4, 2, 4, 4
R = 8
J = 32
RJ = R * J
CH = 128
TB = 256
TAU = TB // R
SLOTS = 16
ZL = 64
ND = ZL // R + 1
KW = 128 + ND * RJ
PX = R * CH
KP = 16 * J
G = 16
ROWS = 256
XROWS = 3 * ROWS


F32 = jnp.float32
BF16 = jnp.bfloat16
VMEM = pltpu.VMEM
ANY = pl.ANY


def small_params():
    return pltpu.CompilerParams(vmem_limit_bytes=12 << 20)


def smem_spec():
    return pl.BlockSpec(memory_space=pltpu.SMEM)


def vmem_spec():
    return pl.BlockSpec(memory_space=pltpu.VMEM)


def prep_kernel(idx, s_hbm, k_hbm, t_hbm, own_ref, oth_ref, o_ref, s_ref, k_ref, t_ref, g_ref, f_ref, sem):
    x, c = idx[0], idx[1]
    rows = pl.ds(pl.multiple_of(c * CH, CH), CH)
    get_s = pltpu.make_async_copy(s_hbm.at[0], s_ref, sem.at[4])
    get_t = pltpu.make_async_copy(t_hbm.at[0], t_ref, sem.at[5])
    get_k = [
        pltpu.make_async_copy(
            k_hbm.at[pl.ds(4 * q, 4), rows, :], k_ref.at[pl.ds(4 * q, 4)], sem.at[q]
        )
        for q in range(4)
    ]
    for cp in (get_s, get_t, *get_k):
        cp.start()

    get_s.wait()
    g_ref[0] = s_ref[:, :CH].astype(F32)
    g_ref[1] = s_ref[:, CH:].astype(F32)
    for p in range(R):
        lo = g_ref[0, pl.ds(p, TAU, stride=R), :]
        hi = g_ref[1, pl.ds(p, TAU, stride=R), :]
        first = c == 0
        own_ref[:, p * CH : (p + 1) * CH] = jnp.where(first, lo, hi).astype(BF16)
        oth_ref[:, p * CH : (p + 1) * CH] = jnp.where(first, hi, lo).astype(BF16)

    get_t.wait()
    group = lane_groups((TAU, 128))
    for y in range(NY):
        f_ref[y] = t_ref[:, y * 128 : (y + 1) * 128].astype(F32)
        for q in range(2):
            v = [f_ref[y, pl.ds(4 * q + i, TAU, stride=R), :] for i in range(4)]
            for i, out in enumerate(regroup(v, group)):
                o_ref[y, i * TAU : (i + 1) * TAU, KP + q * 128 : KP + (q + 1) * 128] = out.astype(BF16)

    group = lane_groups((CH, 128))
    for q in range(4):
        get_k[q].wait()
        for y in range(NY):
            out = None
            for i in range(4):
                v = k_ref[4 * q + i, :, y * 128 : (y + 1) * 128]
                v = pltpu.roll(v, ((i - x) & 3) * J, 1)
                out = v if out is None else jnp.where(group == i, v, out)
            o_ref[y, :, q * 128 : (q + 1) * 128] = out


def prep(idx, s, k, t):
    return pl.pallas_call(
        prep_kernel,
        out_shape=(
            jax.ShapeDtypeStruct((TAU, PX), BF16),
            jax.ShapeDtypeStruct((TAU, PX), BF16),
            jax.ShapeDtypeStruct((NY, CH, KP + RJ), BF16),
        ),
        in_specs=[smem_spec()] + [pl.BlockSpec(memory_space=ANY)] * 3,
        out_specs=(vmem_spec(),) * 3,
        scratch_shapes=[
            VMEM((TB, 2 * CH), BF16),
            VMEM((16, CH, 512), BF16),
            VMEM((TB, 512), BF16),
            VMEM((2, TB, CH), F32),
            VMEM((NY, TB, 128), F32),
            pltpu.SemaphoreType.DMA((6,)),
        ],
        compiler_params=pltpu.CompilerParams(vmem_limit_bytes=60 << 20),
        cost_estimate=cost(1 << 9),
        name="prep",
    )(idx, s, k, t)


def part_kernel(idx, r_ref, k_ref, *t_refs):
    k_ref[...] = r_ref[:, :, :KP]
    for e in range(NX):
        rows = pl.ds(pl.multiple_of(((idx[0] + e) & 3) * TAU, TAU), TAU)
        t_refs[e][...] = r_ref[:, rows, KP:]


def part(idx, r):
    return pl.pallas_call(
        part_kernel,
        out_shape=(jax.ShapeDtypeStruct((NY, CH, KP), BF16),)
        + (jax.ShapeDtypeStruct((NY, TAU, RJ), BF16),) * NX,
        in_specs=[smem_spec(), vmem_spec()],
        out_specs=(vmem_spec(),) * (1 + NX),
        compiler_params=small_params(),
        cost_estimate=cost(1 << 9),
        name="part",
    )(idx, r)


def lane_groups(shape):
    return lax.broadcasted_iota(jnp.int32, shape, len(shape) - 1) // J


def regroup(blocks, group):
    out = []
    for a in range(4):
        acc = None
        for g in range(4):
            shift = (g - a) * J % 128
            v = blocks[g] if shift == 0 else pltpu.roll(blocks[g], shift, 1)
            acc = v if acc is None else jnp.where(group == g, v, acc)
        out.append(acc)
    return out


def expand_rows_kernel(idx, *refs):
    a_refs, b_refs, o_refs = refs[:NY], refs[NY : NY + NX], refs[NY + NX :]
    x = idx[0]
    row = lax.broadcasted_iota(jnp.int32, (XROWS, 1), 0)
    back = 2 - row // ROWS
    step = (row // G) % 16
    g = row % G
    hi = ((x - (g // 2) % 4) & 3) * 4 + (g // 8) * 2 + g % 2 - back
    other = ((hi >> 1) + idx[1]) & 1
    src = other * 128 + ((x - (hi >> 2)) & 3) * 32 + (hi & 1) * 16 + step
    src = jnp.where(hi >= 0, src, -1)
    col = lax.broadcasted_iota(jnp.int32, (XROWS, ROWS), 1)
    pick = jnp.where(src == col, 1.0, 0.0).astype(BF16)
    for d in range(NY):
        for b in range(PX // RJ):
            lanes = slice(b * RJ, (b + 1) * RJ)
            v = [a_refs[d][e, :, lanes] for e in range(NX)]
            v += [b_refs[e][d, :, lanes] for e in range(NX)]
            v = jnp.concatenate(v, axis=0)
            o_refs[d][:, lanes] = jnp.dot(pick, v, preferred_element_type=F32).astype(BF16)


def expand_rows(idx, a, b):
    return pl.pallas_call(
        expand_rows_kernel,
        out_shape=(jax.ShapeDtypeStruct((XROWS, PX), BF16),) * NY,
        in_specs=[smem_spec()] + [vmem_spec()] * (NY + NX),
        out_specs=(vmem_spec(),) * NY,
        compiler_params=small_params(),
        cost_estimate=cost(4 << 9),
        name="expand_rows",
    )(idx, *a, *b)


def cost(kflop):
    return pl.CostEstimate(flops=kflop * 1000000, bytes_accessed=1 << 20, transcendentals=0)


def shift_lags_kernel(*refs):
    n = len(refs) // 2
    lane = lax.broadcasted_iota(jnp.int32, (CH, 128), 1)
    zero = jnp.zeros((CH, 128), BF16)
    for k_ref, o_ref in zip(refs[:n], refs[n:]):
        for s in range(4):
            rows = slice(s * CH, (s + 1) * CH)
            prior = zero
            for b in range(KW // 128):
                if 1 <= b <= 16:
                    q = b - 1
                    v = k_ref[q // 4, :, (q % 4) * 128 : (q % 4 + 1) * 128]
                    if s:
                        v = pltpu.roll(v, J * s, 1)
                else:
                    v = zero
                o_ref[rows, b * 128 : (b + 1) * 128] = jnp.where(lane < J * s, prior, v) if s else v
                prior = v


def shift_lags(*ks):
    return pl.pallas_call(
        shift_lags_kernel,
        out_shape=(jax.ShapeDtypeStruct((4 * CH, KW), BF16),) * len(ks),
        in_specs=[vmem_spec()] * len(ks),
        out_specs=(vmem_spec(),) * len(ks),
        compiler_params=small_params(),
        cost_estimate=cost(len(ks) << 9),
        name="shift_lags",
    )(*ks)


def accumulate(idx, acc_ref, x_refs, k_ref, dist, before):
    zs = (idx[2] - dist) & 3

    lhs, rhs = [], []
    for d in range(ND):
        r0 = pl.multiple_of((32 - 8 * zs - d) * G, G)
        lhs.append(jnp.concatenate([r[pl.ds(r0, ROWS), :] for r in x_refs], axis=0))
        rhs += [k_ref[:, d * RJ + 128 : d * RJ + 128 + RJ], k_ref[:, d * RJ : (d + 1) * RJ]]
    acc = jnp.dot(
        jnp.concatenate(lhs, axis=1), jnp.concatenate(rhs, axis=0), preferred_element_type=F32
    )
    acc_ref[...] = acc if before is None else before[...] + acc


def stage0_kernel(idx, x0, x1, x2, x3, k0, acc_ref):
    accumulate(idx, acc_ref, [x0, x1, x2, x3], k0, 0, None)


def stage1_kernel(idx, a_ref, x0, x1, x2, x3, k1, acc_ref):
    accumulate(idx, acc_ref, [x0, x1, x2, x3], k1, 1, a_ref)


def stage3_kernel(idx, a_ref, x0, x1, x2, x3, k3, acc_ref):
    accumulate(idx, acc_ref, [x0, x1, x2, x3], k3, 3, a_ref)


def stage2_kernel(idx, a_ref, x0, x1, x2, x3, k2, keep_ref, send_ref, acc_ref):
    c = idx[1]
    accumulate(idx, acc_ref, [x0, x1, x2, x3], k2, 2, a_ref)
    for i in range(NY * 16):
        rows = slice(i * 8, (i + 1) * 8)
        keep_ref[rows] = acc_ref[pl.ds(pl.multiple_of(i * G + c * 8, 8), 8), :]
        send_ref[rows] = acc_ref[pl.ds(pl.multiple_of(i * G + 8 - c * 8, 8), 8), :]


def stage(kernel, outs, units, idx, *args, scratch=()):
    return pl.pallas_call(
        kernel,
        out_shape=outs,
        in_specs=[smem_spec()] + [vmem_spec()] * len(args),
        out_specs=jax.tree.map(lambda _: vmem_spec(), outs),
        scratch_shapes=scratch,
        compiler_params=pltpu.CompilerParams(vmem_limit_bytes=16 << 20),
        cost_estimate=cost(units * 2400),
    )(idx, *args)


def errors_kernel(idx, keep_ref, recv_ref, t0, t1, t2, t3, e_ref, b_ref, head_ref, est_ref):
    x, y = idx[0], idx[3]
    for w in range(2):
        lanes = slice(w * 128, (w + 1) * 128)
        est_ref[w] = keep_ref[:, lanes] + recv_ref[:, lanes]
    for d in range(NY):
        for e in range(NX):
            slot = ((y - d) & 3) * NX + ((x - e) & 3)
            for w in range(2):
                lanes = slice(w * 128, (w + 1) * 128)
                est = jnp.concatenate(
                    [est_ref[w, pl.ds(d * 128 + e * 2 + h, 16, stride=8), :] for h in range(2)], axis=0
                )
                v = (t0, t1, t2, t3)[e][(y - d) & 3, :, lanes].astype(F32) - est
                e_ref[d * NX + e, :, lanes] = v
                b_ref[slot, :, lanes] = v.astype(BF16)
                head_ref[d * NX + e, :, lanes] = v[: LAGS // R]


def make_errors(idx, keep, recv, *tgt):
    return pl.pallas_call(
        errors_kernel,
        out_shape=(
            jax.ShapeDtypeStruct((SLOTS, TAU, RJ), F32),
            jax.ShapeDtypeStruct((SLOTS, TAU, RJ), BF16),
            jax.ShapeDtypeStruct((SLOTS, LAGS // R, RJ), F32),
        ),
        in_specs=[smem_spec()] + [vmem_spec()] * 6,
        out_specs=(vmem_spec(),) * 3,
        scratch_shapes=[VMEM((2, TAU * SLOTS, 128), F32)],
        compiler_params=small_params(),
        name="make_errors",
    )(idx, keep, recv, *tgt)


def corr_kernel(idx, e_ref, head_ref, o_ref, ext_ref, d_ref, sh_ref):
    x, c = idx[0], idx[1]
    n = LAGS // R
    last = c == NC - 1
    for i in range(SLOTS):
        e = i % NX
        ext_ref[i, :TAU, :] = e_ref[i]
        after = head_ref[i - e + (e - 1) % NX]
        after = jnp.where(((x - e) & 3) == NX - 1, 0.0, after)
        ext_ref[i, TAU:, :] = jnp.where(last, after, head_ref[i])
    past = jnp.transpose(e_ref[...].reshape(SLOTS * TAU, RJ))
    past_hi = past.astype(BF16)
    past_lo = (past - past_hi.astype(F32)).astype(BF16)
    row = lax.broadcasted_iota(jnp.int32, (RJ, RJ), 0)
    col = lax.broadcasted_iota(jnp.int32, (RJ, RJ), 1)
    same_mode = row % J == col % J
    d_ref[...] = jnp.zeros_like(d_ref)
    for a in range(n + 1):
        fut = ext_ref[:, a : a + TAU, :].reshape(SLOTS * TAU, RJ)
        hi = fut.astype(BF16)
        lo = (fut - hi.astype(F32)).astype(BF16)
        gram = (
            jnp.dot(past_hi, hi, preferred_element_type=F32)
            + jnp.dot(past_hi, lo, preferred_element_type=F32)
            + jnp.dot(past_lo, hi, preferred_element_type=F32)
        )
        gram = jnp.where(same_mode, gram, 0.0)
        for p in range(R):
            d_ref[p, a : a + 1, :] = jnp.sum(gram[p * J : (p + 1) * J], axis=0, keepdims=True)
    lane = lax.broadcasted_iota(jnp.int32, (16, RJ), 1)
    here = jnp.zeros((16, RJ), F32)
    before = jnp.zeros((16, RJ), F32)
    for p in range(R):
        v = d_ref[p]
        if p:
            v = pltpu.roll(v, RJ - J * p, 1)
        stays = lane < RJ - J * p
        here = here + jnp.where(stays, v, 0.0)
        before = before + jnp.where(stays, 0.0, v)
    sh_ref[0:16, :] = before
    sh_ref[16:24, :] = jnp.zeros((8, RJ), F32)
    total = here + sh_ref[1:17, :]
    for i in range(NZ * NC):
        o_ref[i] = total


def lag_sums(idx, e, head):
    return pl.pallas_call(
        corr_kernel,
        out_shape=jax.ShapeDtypeStruct((NZ * NC, 16, RJ), F32),
        in_specs=[smem_spec(), vmem_spec(), vmem_spec()],
        out_specs=vmem_spec(),
        scratch_shapes=[
            VMEM((SLOTS, TAU + LAGS // R, RJ), F32),
            VMEM((R, 16, RJ), F32),
            VMEM((24, RJ), F32),
        ],
        compiler_params=small_params(),
        name="lag_sums",
    )(idx, e, head)


def whiten_kernel(count, s_ref, e_ref, o_ref):
    total = s_ref[0]
    for i in range(1, NZ * NC):
        total = total + s_ref[i]
    lane = lax.broadcasted_iota(jnp.int32, (8, RJ), 1)
    base = jnp.where(lane < J, total[:8], 0.0)[0:1]
    zero_lag = base
    for i in range(1, R):
        zero_lag = zero_lag + pltpu.roll(base, i * J, 1)
    moved = pltpu.roll(total, RJ - J, 1)
    sums = jnp.where(lane < RJ - J, moved[0:8], moved[1:9])
    w = math.sqrt(count) * (sums / count) / (zero_lag / count + EPS)
    hi = w.astype(BF16).astype(F32)
    terms = jnp.concatenate([hi, w - hi], axis=0).astype(BF16)
    for i in range(SLOTS):
        o_ref[i, :TAU] = e_ref[i]
        o_ref[i, TAU:] = terms


def whiten(sums, errs, count):
    return pl.pallas_call(
        functools.partial(whiten_kernel, count),
        out_shape=jax.ShapeDtypeStruct((SLOTS, TAU + 16, RJ), BF16),
        in_specs=[vmem_spec()] * 2,
        out_specs=vmem_spec(),
        compiler_params=small_params(),
        name="whiten",
    )(sums, errs)


def unpack_kernel(r_ref, e_ref, w_ref, f_ref):
    for y in range(NY):
        for q in range(2):
            lanes = slice(q * 128, (q + 1) * 128)
            blocks = [r_ref[y * NX + x, :, lanes].astype(F32) for x in range(NX)]
            parts = (
                (0, TAU, [v[:TAU] for v in blocks]),
                (TB, 8, [v[TAU : TAU + 8] + v[TAU + 8 :] for v in blocks]),
            )
            for at, n, v in parts:
                for i, o in enumerate(regroup(v, lane_groups((n, 128)))):
                    f_ref[y, pl.ds(at + 4 * q + i, n, stride=R), :] = o
        e_ref[0, :, y * 128 : (y + 1) * 128] = f_ref[y, :TB].astype(BF16)
        w_ref[:, y * 128 : (y + 1) * 128] = f_ref[y, TB:]


def unpack(r):
    return pl.pallas_call(
        unpack_kernel,
        out_shape=(
            jax.ShapeDtypeStruct((1, TB, 512), BF16),
            jax.ShapeDtypeStruct((LAGS, 512), F32),
        ),
        in_specs=[vmem_spec()],
        out_specs=(vmem_spec(), vmem_spec()),
        scratch_shapes=[VMEM((NY, TB + LAGS, 128), F32)],
        compiler_params=small_params(),
        name="unpack",
    )(r)


def shift_by(v, axis, by):
    n = lax.axis_size(axis)
    return lax.ppermute(v, axis, [(i, (i + by) % n) for i in range(n)])


def gather_ring(v, axis):
    out = [v]
    for by in (1, 2, -1):
        out.append(shift_by(v, axis, by))
    return out


def body(sensors, kernel, target):
    x, c, z, y = (lax.axis_index(a) for a in ("x", "c", "z", "y"))
    idx = jnp.stack([x, c, z, y]).astype(jnp.int32)
    count = float(16 * 2048)

    own, oth, pieces = prep(idx, sensors, kernel, target)
    got = shift_by(oth, "c", 1)
    row = jnp.stack(gather_ring(own, "x"))
    pieces = lax.all_to_all(pieces, "y", 0, 0)
    column = jnp.stack(gather_ring(got, "y"))
    mine, *tgt = part(idx, pieces)
    rows = gather_ring(row, "y")
    columns = gather_ring(column, "x")
    ks = gather_ring(mine, "z")
    for e in range(1, NX):
        tgt[e] = shift_by(tgt[e], "x", e)

    (k0,) = shift_lags(mine)
    xs = expand_rows(idx, rows, columns)
    whole = jax.ShapeDtypeStruct((4 * ROWS, RJ), F32)
    acc = stage(stage0_kernel, whole, 4, idx, *xs, k0)
    (k1,) = shift_lags(ks[1])
    acc = stage(stage1_kernel, whole, 4, idx, acc, *xs, k1)
    (k3,) = shift_lags(ks[3])
    acc = stage(stage3_kernel, whole, 4, idx, acc, *xs, k3)
    (k2,) = shift_lags(ks[2])
    half = jax.ShapeDtypeStruct((2 * ROWS, RJ), F32)
    keep, send = stage(
        stage2_kernel, (half, half), 4, idx, acc, *xs, k2, scratch=[VMEM((4 * ROWS, RJ), F32)]
    )
    recv = shift_by(send, "c", 1)
    e, errs, head = make_errors(idx, keep, recv, *tgt)
    next_head = shift_by(head, "c", 1)
    sums = lax.all_to_all(lag_sums(idx, e, next_head), ("z", "c"), 0, 0)
    return unpack(lax.all_to_all(whiten(sums, errs, count), ("y", "x"), 0, 0))


def solution(mesh):
    split = Mesh(mesh.devices.reshape(NX, NC, NZ, NY), ("x", "c", "z", "y"))
    member, tm = ("z", "y"), ("x", "c")
    in_specs = (P(member, tm, None), P(member, None, None), P(member, tm, None))
    out_specs = (P(member, tm, None), P())
    return jax.shard_map(body, mesh=split, in_specs=in_specs, out_specs=out_specs, check_vma=False)
```
